256 devices in a mesh: tm: 4 (over y), mp: 4 (over x_hi, core), section: 16 (over z, x_lo).
Axes of the slice: x: 4 (x_hi: 2, x_lo: 2; x = x_hi * 2 + x_lo), y: 4, z: 8, core: 2. Of those that a mesh axis runs over, the one named last changes fastest.
Arguments:
- mel_frames: bfloat16 [32768, 128], P(('tm', 'section')), may hold values from -6 to 6
- conv1_weight: bfloat16 [3, 128, 1280], P(None, None, 'mp'), may hold values from -0.3125 to 0.3125
- conv2_weight: bfloat16 [3, 1280, 1280], P(None, 'section', 'mp'), may hold values from -0.09375 to 0.09375
- attn_gain: float32 [1280], P('mp'), may hold values from 0.1 to 1.9
- qkv_weight: bfloat16 [1280, 3, 1024], P('section', None, 'mp')
- out_weight: bfloat16 [1024, 1280], P('mp'), may hold values from -0.1875 to 0.1875
- post_gain: float32 [1280], P('mp'), may hold values from 0.1 to 1.9
- proj_weight: bfloat16 [1280, 4096], P('section', 'mp'), may hold values from -0.15625 to 0.15625
- rms_gain: float32 [4096], P('mp'), may hold values from 0.1 to 1.9
- kv_weight: bfloat16 [4096, 4096], P(('mp', 'section')), may hold values from -0.09375 to 0.09375
Outputs:
- kv_cache: bfloat16 [8192, 4096], P(('tm', 'section'), 'mp')
The draws below stay inside these ranges and needn't reach their ends.
All inputs are finite; a program needn't handle non-finite values.
Results may differ from the reference program's by a relative error of at most 0.04.
Values may be sent and summed in bfloat16 or wider, within the bound.
A program may use at most 64 MiB of HBM per device.

```python
import math
import jax
import jax.numpy as jnp
from jax import lax

D = 1280
MEL = 128
H_ENC = 16
HD = 64
DL = 4096
KVH = 16
LHD = 128
QW = 1024
KVC = 4096
FRAMES = 16384
MEL_FRAMES = 32768
POOLED = 8192


def draw_qkv_weight(key, part):
    base = jax.random.normal(key, (D, 3, QW), jnp.float32) * D ** (-0.5)
    return base.astype(jnp.bfloat16)


def shard_levels(key, extent, cuts, smallest, high):
    level, own = 1.0, jax.random.fold_in(key, 6)
    for axis_at, parts in cuts:
        heights = jnp.exp(jax.random.uniform(jax.random.fold_in(own, axis_at), (parts,), jnp.float32, smallest / len(cuts), high / len(cuts)))
        level = level * jnp.repeat(heights, extent[axis_at] // parts).reshape([-1 if axis == axis_at else 1 for axis in range(len(extent))])
    return level


def normal_values(stream_key, extent, scale, bound, shards=(), held_as=jnp.bfloat16):
    drawn = scale * jax.random.normal(stream_key, extent, jnp.float32)
    if shards:
        drawn = drawn * shard_levels(stream_key, extent, shards, -0.22, 0.18)
    return jnp.clip(drawn, -bound, bound).astype(held_as)


def setup_inputs(seed: int = 0) -> dict:
    seeds = jax.random.split(jax.random.key(seed), 11)
    mel_frames = normal_values(seeds[0], (MEL_FRAMES, MEL), 1.0, 6.0, ((0, 64),))
    conv1_weight = normal_values(seeds[1], (3, MEL, D), (3 * MEL) ** -0.5, 0.3125, ((2, 4),))
    conv2_weight = normal_values(seeds[2], (3, D, D), (3 * D) ** -0.5, 0.09375, ((1, 16), (2, 4)))
    attn_gain = jnp.clip(1.0 + 0.18 * jax.random.normal(seeds[3], (D,), jnp.float32), 0.1, 1.9)
    qkv_weight = draw_qkv_weight(jax.random.fold_in(seeds[10], 71), 0)
    out_weight = normal_values(seeds[5], (QW, D), QW ** -0.5, 0.1875, ((0, 4),))
    post_gain = jnp.clip(1.0 + 0.18 * jax.random.normal(seeds[6], (D,), jnp.float32), 0.1, 1.9)
    proj_weight = normal_values(seeds[7], (D, DL), D ** -0.5, 0.15625, ((0, 16), (1, 4)))
    rms_gain = jnp.clip(1.0 + 0.18 * jax.random.normal(seeds[8], (DL,), jnp.float32), 0.1, 1.9)
    kv_weight = normal_values(seeds[9], (DL, KVC), DL ** -0.5, 0.09375, ((0, 64),))
    return {"mel_frames": mel_frames, "conv1_weight": conv1_weight, "conv2_weight": conv2_weight, "attn_gain": attn_gain, "qkv_weight": qkv_weight, "out_weight": out_weight, "post_gain": post_gain, "proj_weight": proj_weight, "rms_gain": rms_gain, "kv_weight": kv_weight}


def exact_gelu(values):
    return jax.nn.gelu(values, approximate=False)

def layer_norm(rows, gain):
    center = lax.optimization_barrier(jnp.mean(rows, axis=-1, keepdims=True))
    spread = lax.optimization_barrier(jnp.mean(jnp.square(rows - center), axis=-1, keepdims=True))
    return (rows - center) * lax.rsqrt(spread + 1e-05) * gain

def rotate_keys(cache, row_start, col_start):
    rows_count, cols_count = cache.shape
    positions = (row_start + jnp.arange(rows_count, dtype=jnp.int32)).astype(jnp.float32)
    columns = col_start + jnp.arange(cols_count, dtype=jnp.int32)
    half_size = LHD // 2
    within = columns % LHD % half_size
    freq = jnp.power(10000.0, -2.0 * within.astype(jnp.float32) / LHD)
    angle = positions[:, None] * freq[None, :]
    grouped = cache.reshape(rows_count, cols_count // LHD, 2, half_size)
    partner = jnp.stack([-grouped[:, :, 1], grouped[:, :, 0]], axis=2).reshape(rows_count, cols_count)
    turned = cache * jnp.cos(angle) + partner * jnp.sin(angle)
    return jnp.where((columns < KVH * LHD)[None, :], turned, cache)

def reference(mel_frames, conv1_weight, conv2_weight, attn_gain, qkv_weight, out_weight, post_gain, proj_weight, rms_gain, kv_weight):
    padded = jnp.pad(mel_frames, ((1, 1), (0, 0)))
    first_sum = jnp.dot(padded[0:MEL_FRAMES], conv1_weight[0], preferred_element_type=jnp.float32)
    first_sum = first_sum + jnp.dot(padded[1:MEL_FRAMES + 1], conv1_weight[1], preferred_element_type=jnp.float32)
    first_sum = first_sum + jnp.dot(padded[2:MEL_FRAMES + 2], conv1_weight[2], preferred_element_type=jnp.float32)
    first = exact_gelu(first_sum).astype(jnp.bfloat16)
    extended = jnp.pad(first, ((1, 1), (0, 0)))
    second = jnp.dot(extended[0:MEL_FRAMES:2], conv2_weight[0], preferred_element_type=jnp.float32)
    second = second + jnp.dot(extended[1:MEL_FRAMES + 1:2], conv2_weight[1], preferred_element_type=jnp.float32)
    second = second + jnp.dot(extended[2:MEL_FRAMES + 2:2], conv2_weight[2], preferred_element_type=jnp.float32)
    hidden = exact_gelu(second).astype(jnp.bfloat16)
    normed = layer_norm(hidden.astype(jnp.float32), attn_gain).astype(jnp.bfloat16)
    projected = jnp.dot(normed, qkv_weight.reshape(D, 3 * QW), preferred_element_type=jnp.float32).astype(jnp.bfloat16)
    queries = projected[:, 0:QW].astype(jnp.float32).reshape(FRAMES, H_ENC, HD)
    keys_all = projected[:, QW:2 * QW].astype(jnp.float32).reshape(FRAMES, H_ENC, HD)
    values_all = projected[:, 2 * QW:3 * QW].astype(jnp.float32).reshape(FRAMES, H_ENC, HD)
    block_size = math.gcd(FRAMES, 256)

    def attend(query_block):
        scores = jnp.einsum('qhd,khd->hqk', query_block, keys_all, precision=lax.Precision.HIGHEST) * 0.125
        peak = lax.optimization_barrier(jnp.max(scores, axis=-1, keepdims=True))
        weights = jnp.exp(scores - peak)
        totals = lax.optimization_barrier(jnp.sum(weights, axis=-1))
        rounded = lax.optimization_barrier(weights.astype(jnp.bfloat16)).astype(jnp.float32)
        product = jnp.einsum('hqk,khd->qhd', rounded, values_all, precision=lax.Precision.HIGHEST)
        return product / jnp.transpose(totals)[:, :, None]
    attended = lax.map(attend, queries.reshape(FRAMES // block_size, block_size, H_ENC, HD))
    attended = attended.reshape(FRAMES, QW).astype(jnp.bfloat16)
    residual = hidden.astype(jnp.float32) + jnp.dot(attended, out_weight, preferred_element_type=jnp.float32)
    pooled = lax.optimization_barrier(jnp.mean(residual.reshape(POOLED, 2, D), axis=1))
    post = layer_norm(pooled, post_gain).astype(jnp.bfloat16)
    embedded = jnp.dot(post, proj_weight, preferred_element_type=jnp.float32).astype(jnp.bfloat16)
    widened = embedded.astype(jnp.float32)
    squares = lax.optimization_barrier(jnp.mean(widened * widened, axis=-1, keepdims=True))
    scaled = (widened * lax.rsqrt(squares + 1e-06) * rms_gain).astype(jnp.bfloat16)
    cache = jnp.dot(scaled, kv_weight, preferred_element_type=jnp.float32)
    return rotate_keys(cache, 0, 0).astype(jnp.bfloat16)
```

```python
import functools
import math

import jax
import jax.numpy as jnp
from jax import lax
from jax.experimental import pallas as pl
from jax.experimental.pallas import tpu as pltpu
from jax.sharding import PartitionSpec as P

D = 1280
HD = 64
DL = 4096
KVH = 16
LHD = 128
MESH = pl.DeviceIdType.MESH
F32 = jnp.float32
BF16 = jnp.bfloat16


def extended_2(cells, sides, width):
    for axis, dim in sides:
        count = lax.axis_size(axis)
        ends = count - 1
        head = lax.slice_in_dim(cells, 0, width, axis=dim)
        tail = lax.slice_in_dim(cells, cells.shape[dim] - width, cells.shape[dim], axis=dim)
        cells = jnp.concatenate(
            [
                lax.ppermute(tail, axis, [(i, (i + 1) % count) for i in range(ends)]),
                cells,
                lax.ppermute(head, axis, [((i + 1) % count, i) for i in range(ends)]),
            ],
            axis=dim,
        )
    return cells


def shifted(value, axis, steps):
    count = lax.axis_size(axis)
    initial, last = (max(0, -steps), min(count, count - steps))
    return lax.ppermute(value, axis, [(source, source + steps) for source in range(initial, last)])


def exact_gelu(values):
    return jax.nn.gelu(values, approximate=False)


def spread_norm(rows, gain):
    sum_rows, sum_squares = lax.psum((jnp.sum(rows, axis=-1), jnp.sum(rows * rows, axis=-1)), "mp")
    center = sum_rows / D
    spread = sum_squares / D - center * center
    return (rows - center[:, None]) * lax.rsqrt(spread[:, None] + 1e-05) * gain


def rotate_keys(cache, row_start, col_start):
    rows_count, cols_count = cache.shape
    positions = (row_start + jnp.arange(rows_count, dtype=jnp.int32)).astype(jnp.float32)
    columns = col_start + jnp.arange(cols_count, dtype=jnp.int32)
    half_size = LHD // 2
    within = columns % LHD % half_size
    freq = jnp.power(10000.0, -2.0 * within.astype(jnp.float32) / LHD)
    angle = positions[:, None] * freq[None, :]
    grouped = cache.reshape(rows_count, cols_count // LHD, 2, half_size)
    partner = jnp.stack([-grouped[:, :, 1], grouped[:, :, 0]], axis=2).reshape(
        rows_count, cols_count
    )
    turned = cache * jnp.cos(angle) + partner * jnp.sin(angle)
    return jnp.where((columns < KVH * LHD)[None, :], turned, cache)


def place():
    mp, sec = lax.axis_index("mp"), lax.axis_index("section")
    return lax.axis_index("tm"), mp // 2, mp % 2, sec // 2, sec % 2


def device(y, x_hi, c, z, x_lo):
    return {"tm": y, "mp": x_hi * 2 + c, "section": z * 2 + x_lo}


def remote(src, dst, send, recv, target):
    return pltpu.make_async_remote_copy(
        src_ref=src, dst_ref=dst, send_sem=send, recv_sem=recv, device_id=target, device_id_type=MESH
    )


NEG = -1e30
TQ = 256


def attn_kernel(
    pk, out, kv, qbox, qs, m, l, acc, obuf, obox,
    kv_s, kv_r, q_s, q_r, o_s, o_r, loc, up_s, up_r, dn_s, dn_r, co_s, co_r,
):
    y, x_hi, c, z, x_lo = place()
    Z = kv.shape[0]
    n = qbox.shape[0]
    up = device(y, x_hi, c, lax.rem(z + 1, Z), x_lo)
    down = device(y, x_hi, c, lax.rem(z + Z - 1, Z), x_lo)
    twin = device(y, x_hi, 1 - c, z, x_lo)
    peers = [device(i, x_hi, x_lo, z, c) for i in range(n)]
    mirror = c == x_lo

    barrier = pltpu.get_barrier_semaphore()
    for who in (up, down, twin):
        pl.semaphore_signal(barrier, inc=1, device_id=who, device_id_type=MESH)
    for i in range(n):
        own = jnp.logical_and(mirror, y == i)

        @pl.when(jnp.logical_not(own))
        def _():
            pl.semaphore_signal(barrier, inc=1, device_id=peers[i], device_id_type=MESH)

    pl.semaphore_wait(barrier, 3 + n - mirror.astype(jnp.int32))

    half = kv.shape[2] // n
    for i in range(n):
        own = jnp.logical_and(mirror, y == i)
        rows = pl.ds(pl.multiple_of(y * half, half), half)

        @pl.when(jnp.logical_not(own))
        def _():
            remote(pk.at[i, 0:half], kv.at[z, x_lo, rows], kv_s.at[i], kv_r.at[y], peers[i]).start()
            remote(pk.at[i, half:], qbox.at[y], q_s.at[i], q_r.at[y], peers[i]).start()

        @pl.when(own)
        def _():
            pltpu.make_async_copy(pk.at[i, 0:half], kv.at[z, c, rows], loc.at[0]).start()
            pltpu.make_async_copy(pk.at[i, half:], qbox.at[y], loc.at[1]).start()

    m[...] = jnp.full(m.shape, NEG, F32)
    l[...] = jnp.zeros(l.shape, F32)
    acc[...] = jnp.zeros(acc.shape, F32)

    for i in range(n):
        own = jnp.logical_and(mirror, y == i)
        rows = pl.ds(i * half, half)

        @pl.when(jnp.logical_not(own))
        def _():
            remote(pk.at[i, 0:half], kv.at[z, c, rows], kv_s.at[i], kv_r.at[i], peers[i]).wait()
            remote(pk.at[i, half:], qbox.at[i], q_s.at[i], q_r.at[i], peers[i]).wait()

        @pl.when(own)
        def _():
            pltpu.make_async_copy(pk.at[i, 0:half], kv.at[z, c, rows], loc.at[0]).wait()
            pltpu.make_async_copy(pk.at[i, half:], qbox.at[i], loc.at[1]).wait()

    def block(ref_z, core):
        return kv.at[ref_z, core]

    def send_up(t, zz):
        return remote(block(zz, c), block(zz, c), up_s.at[t], up_r.at[t], up)

    def send_down(t, zz):
        return remote(block(zz, c), block(zz, c), dn_s.at[t], dn_r.at[t], down)

    def share(k, zz):
        return remote(block(zz, c), block(zz, c), co_s.at[k], co_r.at[k], twin)

    def taken(k, zz):
        return remote(block(zz, 1 - c), block(zz, 1 - c), co_s.at[k], co_r.at[k], twin)

    send_up(0, z).start()
    send_down(0, z).start()
    share(0, z).start()

    lanes = lax.broadcasted_iota(jnp.int32, (half // 2, 128), 1)
    for i in range(n):
        raw = qbox[i].astype(F32) * 0.125
        qs[i * half : i * half + half // 2, :] = jnp.where(lanes < HD, raw, 0.0).astype(BF16)
        qs[i * half + half // 2 : (i + 1) * half, :] = jnp.where(
            lanes < HD, pltpu.roll(raw, HD, 1), 0.0
        ).astype(BF16)

    total = qs.shape[0]

    def process(zz, core):
        def tile(k, carry):
            rows = pl.ds(pl.multiple_of(k * TQ, TQ), TQ)
            pairs = kv[zz, core]
            s = lax.dot_general(
                qs[rows, :], pairs, (((1,), (1,)), ((), ())), preferred_element_type=F32
            )
            old = m[rows, :]
            new = jnp.maximum(old, jnp.max(s, axis=1, keepdims=True))
            m[rows, :] = new
            decay = jnp.exp(old - new)
            w = jnp.exp(s - new[:, 0:1])
            l[rows, :] = l[rows, :] * decay + jnp.sum(w, axis=1, keepdims=True)
            acc[rows, :] = acc[rows, :] * decay + jnp.dot(
                w.astype(BF16), pairs, preferred_element_type=F32
            )
            return carry

        lax.fori_loop(0, total // TQ, tile, 0)

    process(z, c)
    taken(0, z).wait_recv()
    process(z, 1 - c)
    far = Z // 2
    for t in range(1, far + 1):
        below = lax.rem(z + Z - t, Z)
        above = lax.rem(z + t, Z)
        send_up(t - 1, below).wait_recv()
        if t < far:
            send_up(t, below).start()
        share(2 * t - 1, below).start()
        if t < far:
            send_down(t - 1, above).wait_recv()
            if t < far - 1:
                send_down(t, above).start()
            share(2 * t, above).start()
        process(below, c)
        if t < far:
            process(above, c)
        taken(2 * t - 1, below).wait_recv()
        process(below, 1 - c)
        if t < far:
            taken(2 * t, above).wait_recv()
            process(above, 1 - c)

    lane_q = lax.broadcasted_iota(jnp.int32, (half // 2, 128), 1)
    for i in range(n):
        top = pl.ds(i * half, half // 2)
        low = pl.ds(i * half + half // 2, half // 2)
        first = pltpu.roll(acc[top, :] / l[top, :], HD, 1)
        second = acc[low, :] / l[low, :]
        obuf[i] = jnp.where(lane_q < HD, first, second).astype(BF16)
    for i in range(n):
        own = jnp.logical_and(mirror, y == i)

        @pl.when(jnp.logical_not(own))
        def _():
            remote(obuf.at[i], obox.at[y], o_s.at[i], o_r.at[y], peers[i]).start()

        @pl.when(own)
        def _():
            pltpu.make_async_copy(obuf.at[i], obox.at[y], loc.at[0]).start()

    for t in range(far):
        send_up(t, z).wait_send()
    for t in range(far - 1):
        send_down(t, z).wait_send()
    for k in range(2 * far):
        share(k, z).wait_send()

    for i in range(n):
        own = jnp.logical_and(mirror, y == i)

        @pl.when(jnp.logical_not(own))
        def _():
            remote(obuf.at[i], obox.at[i], o_s.at[i], o_r.at[i], peers[i]).wait()

        @pl.when(own)
        def _():
            pltpu.make_async_copy(obuf.at[i], obox.at[i], loc.at[0]).wait()

    for pair in range(n // 2):
        a = obox[2 * pair].astype(F32)
        b = obox[2 * pair + 1].astype(F32)
        cols = slice(pair * 128, (pair + 1) * 128)
        out[0 : half // 2, cols] = jnp.where(lane_q < HD, a, pltpu.roll(b, HD, 1)).astype(BF16)
        out[half // 2 :, cols] = jnp.where(lane_q < HD, pltpu.roll(a, HD, 1), b).astype(BF16)


def attention(projected, heads):
    frames = projected.shape[0]
    n = heads
    Z = lax.axis_size("section") // 2
    split = projected.reshape(frames, 3, heads, HD)
    kvp = jnp.concatenate([split[:, 1], split[:, 2]], axis=-1).transpose(1, 0, 2)
    q = split[:, 0].transpose(1, 0, 2)
    qp = jnp.concatenate([q[:, : frames // 2], q[:, frames // 2 :]], axis=-1)
    pk = jnp.concatenate([kvp, qp], axis=1)
    total = frames * n
    dma = pltpu.SemaphoreType.DMA
    vm = pl.BlockSpec(memory_space=pltpu.VMEM)
    return pl.pallas_call(
        attn_kernel,
        out_shape=jax.ShapeDtypeStruct((frames, heads * HD), BF16),
        in_specs=[vm],
        out_specs=vm,
        scratch_shapes=[
            pltpu.VMEM((Z, 2, total, 128), BF16),
            pltpu.VMEM((n, frames // 2, 128), BF16),
            pltpu.VMEM((total, 128), BF16),
            pltpu.VMEM((total, 128), F32),
            pltpu.VMEM((total, 128), F32),
            pltpu.VMEM((total, 128), F32),
            pltpu.VMEM((n, frames // 2, 128), BF16),
            pltpu.VMEM((n, frames // 2, 128), BF16),
            dma((n,)), dma((n,)), dma((n,)), dma((n,)), dma((n,)), dma((n,)), dma((2,)),
            dma((Z // 2,)), dma((Z // 2,)), dma((Z // 2,)), dma((Z // 2,)), dma((Z,)), dma((Z,)),
        ],
        compiler_params=pltpu.CompilerParams(
            collective_id=1, has_side_effects=True, vmem_limit_bytes=40 * 2**20
        ),
        cost_estimate=pl.CostEstimate(
            flops=4 * total * total * 16 * 64, bytes_accessed=4 * 2**20, transcendentals=total * total * 16
        ),
    )(pk)


def shards(
    mel_frames,
    conv1_weight,
    conv2_weight,
    attn_gain,
    qkv_weight,
    out_weight,
    post_gain,
    proj_weight,
    rms_gain,
    kv_weight,
):
    conv2_full, qkv_full, proj_full, kv_full = (
        lax.all_gather(conv2_weight, "section", axis=1, tiled=True),
        lax.all_gather(qkv_weight, "section", axis=0, tiled=True),
        lax.all_gather(proj_weight, "section", axis=0, tiled=True),
        lax.all_gather(kv_weight, "section", axis=0, tiled=True),
    )
    frames_local = mel_frames.shape[0]
    encoded = frames_local // 2
    channels = conv1_weight.shape[2]
    padded = extended_2(mel_frames, ((("tm", "section"), 0),), 1)
    first_sum = jnp.dot(padded[0:frames_local], conv1_weight[0], preferred_element_type=jnp.float32)
    first_sum = first_sum + jnp.dot(
        padded[1 : frames_local + 1], conv1_weight[1], preferred_element_type=jnp.float32
    )
    first_sum = first_sum + jnp.dot(
        padded[2 : frames_local + 2], conv1_weight[2], preferred_element_type=jnp.float32
    )
    first = exact_gelu(first_sum).astype(jnp.bfloat16)
    before = shifted(first[frames_local - 1 :], ("tm", "section"), 1)
    extended = jnp.concatenate([before, first], axis=0)
    piece = lax.all_gather(extended, "mp", axis=1, tiled=True)
    state = jnp.dot(piece[0:frames_local:2], conv2_full[0], preferred_element_type=jnp.float32)
    state = state + jnp.dot(
        piece[1 : frames_local + 1 : 2], conv2_full[1], preferred_element_type=jnp.float32
    )
    second = state + jnp.dot(
        piece[2 : frames_local + 2 : 2], conv2_full[2], preferred_element_type=jnp.float32
    )
    hidden = exact_gelu(second).astype(jnp.bfloat16)
    normed = spread_norm(hidden.astype(jnp.float32), attn_gain).astype(jnp.bfloat16)
    qkv_cols = qkv_full.shape[1] * qkv_full.shape[2]
    piece = lax.all_gather(normed, "mp", axis=1, tiled=True)
    weight_rows = qkv_full.reshape(piece.shape[1], qkv_cols)
    projected = jnp.dot(piece, weight_rows, preferred_element_type=jnp.float32).astype(jnp.bfloat16)
    width = qkv_full.shape[2]
    heads = width // HD
    attended = attention(projected, heads)
    mixed = lax.psum_scatter(
        jnp.dot(attended, out_weight, preferred_element_type=jnp.float32).astype(jnp.bfloat16),
        "mp",
        scatter_dimension=1,
        tiled=True,
    ).astype(jnp.float32)
    residual = hidden.astype(jnp.float32) + mixed
    pooled_rows = encoded // 2
    pooled = jnp.mean(residual.reshape(pooled_rows, 2, channels), axis=1)
    post = spread_norm(pooled, post_gain).astype(jnp.bfloat16)
    weight_rows = proj_full
    embedded = jnp.dot(
        lax.all_gather(post, "mp", axis=1, tiled=True),
        weight_rows,
        preferred_element_type=jnp.float32,
    ).astype(jnp.bfloat16)
    widened = embedded.astype(jnp.float32)
    squares = lax.psum(jnp.sum(widened * widened, axis=-1), "mp")
    scaled = (widened * lax.rsqrt(squares[:, None] / DL + 1e-06) * rms_gain).astype(jnp.bfloat16)
    cache = lax.psum_scatter(
        jnp.dot(scaled, kv_full, preferred_element_type=jnp.float32).astype(jnp.bfloat16),
        "mp",
        scatter_dimension=1,
        tiled=True,
    ).astype(jnp.float32)
    row_start = (
        lax.axis_index("tm") * lax.axis_size("section") + lax.axis_index("section")
    ) * pooled_rows
    col_start = lax.axis_index("mp") * cache.shape[1]
    return rotate_keys(cache, row_start, col_start).astype(jnp.bfloat16)


def solution(mesh):
    return jax.shard_map(
        shards,
        mesh=mesh,
        in_specs=(
            P(("tm", "section"), None),
            P(None, None, "mp"),
            P(None, "section", "mp"),
            P("mp"),
            P("section", None, "mp"),
            P("mp", None),
            P("mp"),
            P("section", "mp"),
            P("mp"),
            P(("mp", "section"), None),
        ),
        out_specs=P(("tm", "section"), "mp"),
        check_vma=False,
    )
```

```python
import functools
import math

import jax
import jax.numpy as jnp
from jax import lax
from jax.experimental import pallas as pl
from jax.experimental.pallas import tpu as pltpu
from jax.sharding import PartitionSpec as P

D = 1280
HD = 64
DL = 4096
KVH = 16
LHD = 128
MESH = pl.DeviceIdType.MESH
F32 = jnp.float32
BF16 = jnp.bfloat16


def extended_2(cells, sides, width):
    for axis, dim in sides:
        count = lax.axis_size(axis)
        ends = count - 1
        head = lax.slice_in_dim(cells, 0, width, axis=dim)
        tail = lax.slice_in_dim(cells, cells.shape[dim] - width, cells.shape[dim], axis=dim)
        cells = jnp.concatenate(
            [
                lax.ppermute(tail, axis, [(i, (i + 1) % count) for i in range(ends)]),
                cells,
                lax.ppermute(head, axis, [((i + 1) % count, i) for i in range(ends)]),
            ],
            axis=dim,
        )
    return cells


def shifted(value, axis, steps):
    count = lax.axis_size(axis)
    initial, last = (max(0, -steps), min(count, count - steps))
    return lax.ppermute(value, axis, [(source, source + steps) for source in range(initial, last)])


def exact_gelu(values):
    return jax.nn.gelu(values, approximate=False)


def spread_norm(rows, gain):
    sum_rows, sum_squares = lax.psum((jnp.sum(rows, axis=-1), jnp.sum(rows * rows, axis=-1)), "mp")
    center = sum_rows / D
    spread = sum_squares / D - center * center
    return (rows - center[:, None]) * lax.rsqrt(spread[:, None] + 1e-05) * gain


def rotate_keys(cache, row_start, col_start):
    rows_count, cols_count = cache.shape
    positions = (row_start + jnp.arange(rows_count, dtype=jnp.int32)).astype(jnp.float32)
    columns = col_start + jnp.arange(cols_count, dtype=jnp.int32)
    half_size = LHD // 2
    within = columns % LHD % half_size
    freq = jnp.power(10000.0, -2.0 * within.astype(jnp.float32) / LHD)
    angle = positions[:, None] * freq[None, :]
    grouped = cache.reshape(rows_count, cols_count // LHD, 2, half_size)
    partner = jnp.stack([-grouped[:, :, 1], grouped[:, :, 0]], axis=2).reshape(
        rows_count, cols_count
    )
    turned = cache * jnp.cos(angle) + partner * jnp.sin(angle)
    return jnp.where((columns < KVH * LHD)[None, :], turned, cache)


def place():
    mp, sec = lax.axis_index("mp"), lax.axis_index("section")
    return lax.axis_index("tm"), mp // 2, mp % 2, sec // 2, sec % 2


def device(y, x_hi, c, z, x_lo):
    return {"tm": y, "mp": x_hi * 2 + c, "section": z * 2 + x_lo}


def remote(src, dst, send, recv, target):
    return pltpu.make_async_remote_copy(
        src_ref=src, dst_ref=dst, send_sem=send, recv_sem=recv, device_id=target, device_id_type=MESH
    )


NEG = -1e30
TQ = 256
H0 = 32


def greet(Z, Y):
    y, x_hi, c, z, x_lo = place()
    barrier = pltpu.get_barrier_semaphore()
    for step in (1, Z - 1):
        pl.semaphore_signal(
            barrier, inc=1, device_id=device(y, x_hi, c, lax.rem(z + step, Z), x_lo), device_id_type=MESH
        )
    for dy in range(Y):
        for k in range(8):
            if dy == 0 and k == 0:
                continue
            a, b, d = k // 4, (k // 2) % 2, k % 2
            other = device(
                lax.rem(y + dy, Y), lax.rem(x_hi + a, 2), lax.rem(c + b, 2), z, lax.rem(x_lo + d, 2)
            )
            pl.semaphore_signal(barrier, inc=1, device_id=other, device_id_type=MESH)
    pl.semaphore_wait(barrier, 8 * Y + 1)


class Across:
    def __init__(self, src, buf, send, recv):
        y, x_hi, c, z, x_lo = place()
        self.buf, self.send, self.recv, self.src = buf, send, recv, src
        self.me, self.twin, self.far, self.both = (
            x_hi * 2 + c, x_hi * 2 + 1 - c, (1 - x_hi) * 2 + c, (1 - x_hi) * 2 + 1 - c
        )
        self.to_twin = device(y, x_hi, 1 - c, z, x_lo)
        self.to_far = device(y, 1 - x_hi, c, z, x_lo)

    def copy(self, k, src, slot, target):
        return remote(src, self.buf.at[slot], self.send.at[k], self.recv.at[k], target)

    def start(self):
        self.copy(1, self.src, self.me, self.to_far).start()
        self.copy(0, self.src, self.me, self.to_twin).start()

    def relay(self):
        self.copy(1, self.buf.at[self.far], self.far, self.to_far).wait_recv()
        self.copy(2, self.buf.at[self.far], self.far, self.to_twin).start()

    def finish(self):
        self.copy(0, self.buf.at[self.twin], self.twin, self.to_twin).wait_recv()
        self.copy(2, self.buf.at[self.both], self.both, self.to_twin).wait_recv()
        for k in range(3):
            self.copy(k, self.buf.at[self.me], self.me, self.to_twin).wait_send()


class Sections:
    def __init__(self, src, buf, us, ur, ds, dr, ous, our, ods, odr, xs, xr, loc, h0):
        y, x_hi, c, z, x_lo = place()
        self.Z = buf.shape[0]
        self.src, self.buf, self.z, self.x = src, buf, z, x_lo
        self.s = (us, ur, ds, dr, ous, our, ods, odr, xs, xr)
        self.loc = loc
        self.lo = pl.ds(0, h0)
        self.hi = pl.ds(h0, src.shape[0] - h0)
        self.up = device(y, x_hi, c, lax.rem(z + 1, self.Z), x_lo)
        self.down = device(y, x_hi, c, lax.rem(z + self.Z - 1, self.Z), x_lo)
        self.side = device(y, x_hi, c, z, 1 - x_lo)

    def below(self, t):
        return lax.rem(self.z + self.Z - t, self.Z)

    def above(self, t):
        return lax.rem(self.z + t, self.Z)

    def ring(self, kind, t, zz, src=None):
        us, ur, ds, dr, ous, our, ods, odr, xs, xr = self.s
        if kind == "u":
            ref = self.buf.at[zz, self.x]
            return remote(ref if src is None else src, ref, us.at[t], ur.at[t], self.up)
        if kind == "d":
            ref = self.buf.at[zz, self.x]
            return remote(ref if src is None else src, ref, ds.at[t], dr.at[t], self.down)
        ref = self.buf.at[zz, 1 - self.x, self.lo]
        if kind == "ou":
            return remote(ref, ref, ous.at[t], our.at[t], self.up)
        return remote(ref, ref, ods.at[t], odr.at[t], self.down)

    def whole(self, x):
        us, ur, ds, dr, ous, our, ods, odr, xs, xr = self.s
        return remote(self.src, self.buf.at[self.z, x], xs.at[0], xr.at[0], self.side)

    def forward(self, k, zz, x):
        us, ur, ds, dr, ous, our, ods, odr, xs, xr = self.s
        ref = self.buf.at[zz, x, self.hi]
        return remote(ref, ref, xs.at[k], xr.at[k], self.side)

    def local(self):
        return pltpu.make_async_copy(self.src, self.buf.at[self.z, self.x], self.loc)

    def start(self):
        self.local().start()
        self.whole(self.x).start()
        self.ring("u", 0, self.z, self.src).start()
        self.ring("d", 0, self.z, self.src).start()

    def start_other(self):
        self.whole(1 - self.x).wait_recv()
        self.ring("ou", 0, self.z).start()
        self.ring("od", 0, self.z).start()

    def step(self, t):
        far = self.Z // 2
        zz = self.below(t)
        self.ring("u", t - 1, zz).wait_recv()
        if t < far:
            self.ring("u", t, zz).start()
        self.forward(2 * t - 1, zz, self.x).start()
        if t < far:
            zz = self.above(t)
            self.ring("d", t - 1, zz).wait_recv()
            if t < far - 1:
                self.ring("d", t, zz).start()
            self.forward(2 * t, zz, self.x).start()
        self.step_other(t)

    def step_other(self, t):
        far = self.Z // 2
        zz = self.below(t)
        self.ring("ou", t - 1, zz).wait_recv()
        if t < far:
            self.ring("ou", t, zz).start()
            zz = self.above(t)
            self.ring("od", t - 1, zz).wait_recv()
            if t < far - 1:
                self.ring("od", t, zz).start()

    def finish(self):
        far = self.Z // 2
        for t in range(1, far + 1):
            self.forward(2 * t - 1, self.below(t), 1 - self.x).wait_recv()
            if t < far:
                self.forward(2 * t, self.above(t), 1 - self.x).wait_recv()
        self.local().wait()
        self.whole(self.x).wait_send()
        for t in range(far):
            self.ring("u", t, self.z).wait_send()
            self.ring("ou", t, self.z).wait_send()
        for t in range(far - 1):
            self.ring("d", t, self.z).wait_send()
            self.ring("od", t, self.z).wait_send()
        for k in range(1, 2 * far):
            self.forward(k, self.z, self.x).wait_send()


class Quarters:
    def __init__(self, src, buf, us, ur, ds, dr, xs, xr, yus, yur, yds, ydr, rus, rur, rds, rdr, loc):
        y, x_hi, c, z, x_lo = place()
        self.Z, self.Y = buf.shape[0], buf.shape[2]
        self.src, self.buf, self.z, self.x, self.y = src, buf, z, x_lo, y
        self.s = (us, ur, ds, dr, xs, xr, yus, yur, yds, ydr, rus, rur, rds, rdr)
        self.loc = loc
        self.up = device(y, x_hi, c, lax.rem(z + 1, self.Z), x_lo)
        self.down = device(y, x_hi, c, lax.rem(z + self.Z - 1, self.Z), x_lo)
        self.side = device(y, x_hi, c, z, 1 - x_lo)
        self.yn, self.yp = lax.rem(y + 1, self.Y), lax.rem(y + self.Y - 1, self.Y)
        self.yf = lax.rem(y + 2, self.Y)
        self.next = device(self.yn, x_hi, c, z, x_lo)
        self.prev = device(self.yp, x_hi, c, z, x_lo)

    def zs(self, k):
        if k % 2:
            return lax.rem(self.z + self.Z - (k + 1) // 2, self.Z)
        return lax.rem(self.z + k // 2, self.Z)

    def ring(self, kind, t, zz):
        us, ur, ds, dr = self.s[:4]
        ref = self.buf.at[zz, :, self.y]
        if kind == "u":
            return remote(ref, ref, us.at[t], ur.at[t], self.up)
        return remote(ref, ref, ds.at[t], dr.at[t], self.down)

    def cross(self, x):
        xs, xr = self.s[4:6]
        return remote(self.src.at[self.y], self.buf.at[self.z, x, self.y], xs.at[0], xr.at[0], self.side)

    def local(self):
        return pltpu.make_async_copy(self.src, self.buf.at[self.z, self.x], self.loc)

    def spread(self, kind, k, quarter):
        yus, yur, yds, ydr = self.s[6:10]
        if k == 0:
            ref = self.buf.at[self.z, 1 - self.x, quarter]
        else:
            ref = self.buf.at[self.zs(k), :, quarter]
        if kind == "n":
            return remote(ref, ref, yus.at[k], yur.at[k], self.next)
        return remote(ref, ref, yds.at[k], ydr.at[k], self.prev)

    def relay(self, kind, k, quarter):
        rus, rur, rds, rdr = self.s[10:14]
        if kind == "n":
            ref = self.buf.at[self.zs(k), (1 - self.x) if k == 0 else 0, quarter]
            return remote(ref, ref, rus.at[k], rur.at[k], self.next)
        ref = self.buf.at[self.zs(k), 1, quarter]
        return remote(ref, ref, rds.at[k], rdr.at[k], self.prev)

    def start(self):
        self.cross(self.x).start()
        self.local().start()

    def begin(self):
        self.local().wait()
        self.cross(1 - self.x).wait_recv()
        self.spread("n", 0, self.y).start()
        self.spread("p", 0, self.y).start()
        self.ring("u", 0, self.z).start()
        self.ring("d", 0, self.z).start()

    def arrive(self, k):
        far, t, zz = self.Z // 2, (k + 1) // 2, self.zs(k)
        kind = "u" if k % 2 else "d"
        self.ring(kind, t - 1, zz).wait_recv()
        if t < (far if kind == "u" else far - 1):
            self.ring(kind, t, zz).start()
        self.spread("n", k, self.y).start()
        self.spread("p", k, self.y).start()

    def pass_on(self, k):
        self.spread("n", k, self.yp).wait_recv()
        self.relay("n", k, self.yp).start()
        self.spread("p", k, self.yn).wait_recv()
        if k:
            self.relay("p", k, self.yn).start()

    def finish(self):
        far = self.Z // 2
        for k in range(2 * far):
            self.relay("n", k, self.yf).wait_recv()
            if k:
                self.relay("p", k, self.yf).wait_recv()
        self.cross(self.x).wait_send()
        for t in range(far):
            self.ring("u", t, self.z).wait_send()
        for t in range(far - 1):
            self.ring("d", t, self.z).wait_send()
        for k in range(2 * far):
            self.spread("n", k, self.y).wait_send()
            self.spread("p", k, self.y).wait_send()
            self.relay("n", k, self.y).wait_send()
            if k:
                self.relay("p", k, self.y).wait_send()


def normal(rows, gain):
    center = jnp.mean(rows, axis=-1, keepdims=True)
    spread = jnp.mean(jnp.square(rows - center), axis=-1, keepdims=True)
    return (rows - center) * lax.rsqrt(spread + 1e-05) * gain


def tail_kernel(
    pk, hq, ow, pw, kw, pg, rg, cs, sn, out,
    kv, qbox, qs, m, l, acc, obuf, abox, att, res, owf, pwf, kwf, pbox, sbox, keep, tsend, trecv, csend, crecv,
    kv_s, kv_r, q_s, q_r, loc, up_s, up_r, dn_s, dn_r, co_s, co_r, a_s, a_r,
    ow_s, ow_r, pb_s, pb_r, sb_s, sb_r, t_s, t_r, c_s, c_r,
    p0, p1, p2, p3, p4, p5, p6, p7, p8, p9,
    k0, k1, k2, k3, k4, k5, k6, k7, k8, k9, k10, k11, k12, k13,
):
    y, x_hi, c, z, x_lo = place()
    Z = kv.shape[0]
    n = qbox.shape[0]
    me = x_hi * 2 + c
    up = device(y, x_hi, c, lax.rem(z + 1, Z), x_lo)
    down = device(y, x_hi, c, lax.rem(z + Z - 1, Z), x_lo)
    twin = device(y, x_hi, 1 - c, z, x_lo)
    far_dev = device(y, 1 - x_hi, c, z, x_lo)
    peers = [device(i, x_hi, x_lo, z, c) for i in range(n)]
    mirror = c == x_lo
    greet(Z, n)

    outw = Across(ow, owf, ow_s, ow_r)
    proj = Sections(pw, pwf, p0, p1, p2, p3, p4, p5, p6, p7, p8, p9, loc.at[3], H0)
    kvw = Quarters(kw, kwf, k0, k1, k2, k3, k4, k5, k6, k7, k8, k9, k10, k11, k12, k13, loc.at[4])

    half = kv.shape[2] // n
    for i in range(n):
        own = jnp.logical_and(mirror, y == i)
        rows = pl.ds(pl.multiple_of(y * half, half), half)

        @pl.when(jnp.logical_not(own))
        def _():
            remote(pk.at[i, 0:half], kv.at[z, x_lo, rows], kv_s.at[i], kv_r.at[y], peers[i]).start()
            remote(pk.at[i, half:], qbox.at[y], q_s.at[i], q_r.at[y], peers[i]).start()

        @pl.when(own)
        def _():
            pltpu.make_async_copy(pk.at[i, 0:half], kv.at[z, c, rows], loc.at[0]).start()
            pltpu.make_async_copy(pk.at[i, half:], qbox.at[y], loc.at[1]).start()

    kvw.start()
    own_w = pltpu.make_async_copy(ow, owf.at[me], loc.at[5])
    own_w.start()

    m[...] = jnp.full(m.shape, NEG, F32)
    l[...] = jnp.zeros(l.shape, F32)
    acc[...] = jnp.zeros(acc.shape, F32)

    for i in range(n):
        own = jnp.logical_and(mirror, y == i)
        rows = pl.ds(i * half, half)

        @pl.when(jnp.logical_not(own))
        def _():
            remote(pk.at[i, 0:half], kv.at[z, c, rows], kv_s.at[i], kv_r.at[i], peers[i]).wait()
            remote(pk.at[i, half:], qbox.at[i], q_s.at[i], q_r.at[i], peers[i]).wait()

        @pl.when(own)
        def _():
            pltpu.make_async_copy(pk.at[i, 0:half], kv.at[z, c, rows], loc.at[0]).wait()
            pltpu.make_async_copy(pk.at[i, half:], qbox.at[i], loc.at[1]).wait()

    def block(ref_z, core):
        return kv.at[ref_z, core]

    def send_up(t, zz):
        return remote(block(zz, c), block(zz, c), up_s.at[t], up_r.at[t], up)

    def send_down(t, zz):
        return remote(block(zz, c), block(zz, c), dn_s.at[t], dn_r.at[t], down)

    def share(k, zz):
        return remote(block(zz, c), block(zz, c), co_s.at[k], co_r.at[k], twin)

    def taken(k, zz):
        return remote(block(zz, 1 - c), block(zz, 1 - c), co_s.at[k], co_r.at[k], twin)

    send_up(0, z).start()
    send_down(0, z).start()
    share(0, z).start()
    outw.start()

    lanes = lax.broadcasted_iota(jnp.int32, (half // 2, 128), 1)
    for i in range(n):
        raw = qbox[i].astype(F32) * 0.125
        qs[i * half : i * half + half // 2, :] = jnp.where(lanes < HD, raw, 0.0).astype(BF16)
        qs[i * half + half // 2 : (i + 1) * half, :] = jnp.where(
            lanes < HD, pltpu.roll(raw, HD, 1), 0.0
        ).astype(BF16)

    total = qs.shape[0]
    width = kv.shape[2]

    def process(zz, core):
        def tile(k, carry):
            rows = pl.ds(pl.multiple_of(k * TQ, TQ), TQ)
            pairs = kv[zz, core]
            s = lax.dot_general(
                qs[rows, :], pairs, (((1,), (1,)), ((), ())), preferred_element_type=F32
            )
            old = m[rows, :]
            new = jnp.maximum(old, jnp.max(s, axis=1, keepdims=True))
            m[rows, :] = new
            decay = jnp.exp(old - new)
            w = jnp.exp(s - jnp.concatenate([new] * (width // 128), axis=1))
            part = w[:, 0:128]
            for piece in range(1, width // 128):
                part = part + w[:, piece * 128 : (piece + 1) * 128]
            l[rows, :] = l[rows, :] * decay + part
            acc[rows, :] = acc[rows, :] * decay + jnp.dot(
                w.astype(BF16), pairs, preferred_element_type=F32
            )
            return carry

        lax.fori_loop(0, total // TQ, tile, 0)

    kvw.begin()
    process(z, c)
    taken(0, z).wait_recv()
    process(z, 1 - c)
    far = Z // 2
    kvw.pass_on(0)
    for t in range(1, far + 1):
        below = lax.rem(z + Z - t, Z)
        above = lax.rem(z + t, Z)
        send_up(t - 1, below).wait_recv()
        if t < far:
            send_up(t, below).start()
        share(2 * t - 1, below).start()
        if t < far:
            send_down(t - 1, above).wait_recv()
            if t < far - 1:
                send_down(t, above).start()
            share(2 * t, above).start()
        process(below, c)
        kvw.arrive(2 * t - 1)
        if t < far:
            kvw.arrive(2 * t)
        if t > 1:
            kvw.pass_on(2 * t - 3)
            kvw.pass_on(2 * t - 2)
        if t < far:
            process(above, c)
        if t == 1:
            proj.start()
        taken(2 * t - 1, below).wait_recv()
        process(below, 1 - c)
        if t == 2:
            proj.start_other()
            outw.relay()
        if t == 3:
            proj.step(1)
        if t < far:
            taken(2 * t, above).wait_recv()
            process(above, 1 - c)
        if t == 3:
            proj.step(2)
        if t == 4:
            proj.step(3)

    quarter = half // 4
    low = lax.broadcasted_iota(jnp.int32, (quarter // 2, 128), 1) < HD
    head = (x_hi * 2 + x_lo) * n + y

    def give(j, q, slot, sem):
        k = 4 * j + q
        return remote(obuf.at[k], abox.at[slot], a_s.at[k], a_r.at[sem], device(j, q // 2, q % 2, z, c))

    for j in range(n):
        for q in range(4):
            k = 4 * j + q
            at = j * half + q * quarter
            top, bot = pl.ds(at, quarter // 2), pl.ds(at + quarter // 2, quarter // 2)
            first = pltpu.roll(acc[top, :] / jnp.sum(l[top, :], axis=1, keepdims=True), HD, 1)
            second = acc[bot, :] / jnp.sum(l[bot, :], axis=1, keepdims=True)
            obuf[k] = jnp.where(low, first, second).astype(BF16)
    for j in range(n):
        for q in range(4):
            own = jnp.logical_and(mirror, jnp.logical_and(y == j, me == q))

            @pl.when(jnp.logical_not(own))
            def _():
                give(j, q, head, head).start()

            @pl.when(own)
            def _():
                pltpu.make_async_copy(obuf.at[4 * j + q], abox.at[head], loc.at[0]).start()

    proj.step(far)
    kvw.pass_on(2 * far - 1)

    for t in range(far):
        send_up(t, z).wait_send()
    for t in range(far - 1):
        send_down(t, z).wait_send()
    for k in range(2 * far):
        share(k, z).wait_send()
    outw.finish()
    own_w.wait()

    for h in range(4 * n):
        own = jnp.logical_and(mirror, head == h)

        @pl.when(jnp.logical_not(own))
        def _():
            remote(obuf.at[h], abox.at[h], a_s.at[h], a_r.at[h], twin).wait_recv()

        @pl.when(own)
        def _():
            pltpu.make_async_copy(obuf.at[h], abox.at[h], loc.at[0]).wait()

    for pair in range(2 * n):
        a = abox[2 * pair].astype(F32)
        b = abox[2 * pair + 1].astype(F32)
        cols = slice(pair * 128, (pair + 1) * 128)
        att[0 : quarter // 2, cols] = jnp.where(low, a, pltpu.roll(b, HD, 1)).astype(BF16)
        att[quarter // 2 :, cols] = jnp.where(low, pltpu.roll(a, HD, 1), b).astype(BF16)

    mixed = jnp.dot(
        att[...], owf[...].reshape(4 * ow.shape[0], ow.shape[1]), preferred_element_type=F32
    )
    tokens = quarter // 2
    pieces = []
    for k in range(hq.shape[1] // 128):
        at = slice(k * 128, (k + 1) * 128)
        res[k] = hq[:, at].astype(F32) + mixed[:, at]
        pieces.append(
            (res.at[k][pl.ds(0, tokens, stride=2), :] + res.at[k][pl.ds(1, tokens, stride=2), :]) * 0.5
        )
    pooled = jnp.concatenate(pieces, axis=1)
    pbox[me] = normal(pooled, pg[0:1, :]).astype(BF16)
    gather = Across(pbox.at[me], pbox, pb_s, pb_r)
    gather.start()
    gather.relay()
    proj.finish()
    gather.finish()

    post = pbox[...].reshape(4 * tokens, pbox.shape[2])
    embedded = jnp.dot(
        post, pwf[...].reshape(2 * Z * pw.shape[0], pw.shape[1]), preferred_element_type=F32
    ).astype(BF16)
    widened = embedded.astype(F32)
    sbox[me] = jnp.broadcast_to(
        jnp.sum(widened * widened, axis=1, keepdims=True), (4 * tokens, 128)
    )
    squares = Across(sbox.at[me], sbox, sb_s, sb_r)
    squares.start()
    gained = (widened * rg[0:1, :]).astype(BF16)
    cols = pw.shape[1]
    kvw.finish()

    def columns(a, b):
        at = pl.ds(pl.multiple_of((a * 2 + b) * cols, cols), cols)
        return jnp.dot(
            gained, kwf[:, :, :, :, at].reshape(cols, cols), preferred_element_type=F32
        )

    def swap(k):
        return remote(tsend.at[k], trecv.at[k], t_s.at[k], t_r.at[k], twin)

    over = remote(csend, crecv, c_s.at[0], c_r.at[0], far_dev)
    tsend[0] = columns(1 - x_hi, 1 - c).astype(BF16)
    swap(0).start()
    keep[...] = columns(1 - x_hi, c)
    squares.relay()
    swap(0).wait_recv()
    csend[...] = (keep[...] + trecv[0].astype(F32)).astype(BF16)
    over.start()
    tsend[1] = columns(x_hi, 1 - c).astype(BF16)
    swap(1).start()
    keep[...] = columns(x_hi, c)
    squares.finish()
    scale = lax.rsqrt((sbox[0] + sbox[1] + sbox[2] + sbox[3]) / DL + 1e-06)
    swap(1).wait_recv()
    keep[...] = keep[...] + trecv[1].astype(F32)
    over.wait_recv()
    for h in range(cols // LHD):
        at = slice(h * LHD, (h + 1) * LHD)
        value = (keep[:, at] + crecv[:, at].astype(F32)) * scale
        out[:, at] = (value * cs[...] + pltpu.roll(value, HD, 1) * sn[...]).astype(BF16)

    swap(0).wait_send()
    swap(1).wait_send()
    over.wait_send()
    for j in range(n):
        for q in range(4):
            own = jnp.logical_and(mirror, jnp.logical_and(y == j, me == q))

            @pl.when(jnp.logical_not(own))
            def _():
                give(j, q, head, head).wait_send()


def tail(pk, hq, ow, pw, kw, pg, rg, cs, sn):
    n = pk.shape[0]
    frames = pk.shape[1] * 2 // 3
    Z = lax.axis_size("section") // 2
    total = frames * n
    tokens = frames // 2
    quarter = frames // 4
    cols = pw.shape[1]
    sem = pltpu.SemaphoreType.DMA
    vm = pl.BlockSpec(memory_space=pltpu.VMEM)
    V = pltpu.VMEM
    half = Z // 2
    return pl.pallas_call(
        tail_kernel,
        out_shape=jax.ShapeDtypeStruct((tokens, cols), BF16),
        in_specs=[vm] * 9,
        out_specs=vm,
        scratch_shapes=[
            V((Z, 2, total, 128), BF16),
            V((n, tokens, 128), BF16),
            V((total, 128), BF16),
            V((total, 128), F32),
            V((total, 128), F32),
            V((total, 128), F32),
            V((16, quarter // 2, 128), BF16),
            V((16, quarter // 2, 128), BF16),
            V((quarter, ow.shape[0] * 4), BF16),
            V((ow.shape[1] // 128, quarter, 128), F32),
            V((4,) + ow.shape, BF16),
            V((Z, 2) + pw.shape, BF16),
            V((Z, 2) + kw.shape, BF16),
            V((4, quarter // 2, ow.shape[1]), BF16),
            V((4, tokens, 128), F32),
            V((tokens, cols), F32),
            V((2, tokens, cols), BF16),
            V((2, tokens, cols), BF16),
            V((tokens, cols), BF16),
            V((tokens, cols), BF16),
            sem((n,)), sem((n,)), sem((n,)), sem((n,)), sem((6,)),
            sem((half,)), sem((half,)), sem((half,)), sem((half,)), sem((Z,)), sem((Z,)), sem((16,)), sem((16,)),
            sem((3,)), sem((3,)), sem((3,)), sem((3,)), sem((3,)), sem((3,)), sem((2,)), sem((2,)), sem((1,)), sem((1,)),
        ]
        + [sem((half,))] * 8 + [sem((Z,))] * 2
        + [sem((half,))] * 4 + [sem((1,))] * 2 + [sem((Z,))] * 8,
        compiler_params=pltpu.CompilerParams(
            collective_id=1, has_side_effects=True, vmem_limit_bytes=56 * 2**20
        ),
    )(pk, hq, ow, pw, kw, pg, rg, cs, sn)


def pack(projected, heads):
    frames = projected.shape[0]
    split = projected.reshape(frames, 3, heads, HD)
    kvp = jnp.concatenate([split[:, 1], split[:, 2]], axis=-1).transpose(1, 0, 2)
    q = split[:, 0].transpose(1, 0, 2)
    qp = jnp.concatenate([q[:, : frames // 2], q[:, frames // 2 :]], axis=-1)
    return jnp.concatenate([kvp, qp], axis=1)


def tables(rows, cols):
    row_start = (lax.axis_index("tm") * lax.axis_size("section") + lax.axis_index("section")) * rows
    positions = (row_start + jnp.arange(rows, dtype=jnp.int32)).astype(F32)
    within = jnp.arange(LHD, dtype=jnp.int32)
    freq = jnp.power(10000.0, -2.0 * (within % (LHD // 2)).astype(F32) / LHD)
    angle = positions[:, None] * freq[None, :]
    keys = lax.axis_index("mp") * cols < KVH * LHD
    sines = jnp.where(within < LHD // 2, -1.0, 1.0) * jnp.sin(angle)
    return jnp.where(keys, jnp.cos(angle), 1.0), jnp.where(keys, sines, 0.0)


def shards(
    mel_frames,
    conv1_weight,
    conv2_weight,
    attn_gain,
    qkv_weight,
    out_weight,
    post_gain,
    proj_weight,
    rms_gain,
    kv_weight,
):
    conv2_full, qkv_full = (
        lax.all_gather(conv2_weight, "section", axis=1, tiled=True),
        lax.all_gather(qkv_weight, "section", axis=0, tiled=True),
    )
    frames_local = mel_frames.shape[0]
    encoded = frames_local // 2
    channels = conv1_weight.shape[2]
    padded = extended_2(mel_frames, ((("tm", "section"), 0),), 1)
    first_sum = jnp.dot(padded[0:frames_local], conv1_weight[0], preferred_element_type=jnp.float32)
    first_sum = first_sum + jnp.dot(
        padded[1 : frames_local + 1], conv1_weight[1], preferred_element_type=jnp.float32
    )
    first_sum = first_sum + jnp.dot(
        padded[2 : frames_local + 2], conv1_weight[2], preferred_element_type=jnp.float32
    )
    first = exact_gelu(first_sum).astype(jnp.bfloat16)
    before = shifted(first[frames_local - 1 :], ("tm", "section"), 1)
    extended = jnp.concatenate([before, first], axis=0)
    piece = lax.all_gather(extended, "mp", axis=1, tiled=True)
    state = jnp.dot(piece[0:frames_local:2], conv2_full[0], preferred_element_type=jnp.float32)
    state = state + jnp.dot(
        piece[1 : frames_local + 1 : 2], conv2_full[1], preferred_element_type=jnp.float32
    )
    second = state + jnp.dot(
        piece[2 : frames_local + 2 : 2], conv2_full[2], preferred_element_type=jnp.float32
    )
    hidden = exact_gelu(second).astype(jnp.bfloat16)
    normed = spread_norm(hidden.astype(jnp.float32), attn_gain).astype(jnp.bfloat16)
    qkv_cols = qkv_full.shape[1] * qkv_full.shape[2]
    piece = lax.all_gather(normed, "mp", axis=1, tiled=True)
    weight_rows = qkv_full.reshape(piece.shape[1], qkv_cols)
    projected = jnp.dot(piece, weight_rows, preferred_element_type=jnp.float32).astype(jnp.bfloat16)
    width = qkv_full.shape[2]
    heads = width // HD
    pk = pack(projected, heads)
    quarter = encoded // 4
    hq = lax.all_to_all(hidden.reshape(4, quarter, channels), "mp", 0, 0)
    hq = hq.transpose(1, 0, 2).reshape(quarter, 4 * channels)
    gains = lax.all_gather(post_gain.reshape(1, channels), "mp", axis=1, tiled=True)
    cs, sn = tables(encoded // 2, proj_weight.shape[1])
    return tail(
        pk,
        hq,
        out_weight,
        proj_weight,
        kv_weight.reshape(4, kv_weight.shape[0] // 4, kv_weight.shape[1]),
        gains,
        rms_gain.reshape(1, -1),
        cs,
        sn,
    )


def solution(mesh):
    return jax.shard_map(
        shards,
        mesh=mesh,
        in_specs=(
            P(("tm", "section"), None),
            P(None, None, "mp"),
            P(None, "section", "mp"),
            P("mp"),
            P("section", None, "mp"),
            P("mp", None),
            P("mp"),
            P("section", "mp"),
            P("mp"),
            P(("mp", "section"), None),
        ),
        out_specs=P(("tm", "section"), "mp"),
        check_vma=False,
    )
```

```python
import functools
import math

import jax
import jax.numpy as jnp
from jax import lax
from jax.experimental import pallas as pl
from jax.experimental.pallas import tpu as pltpu
from jax.sharding import PartitionSpec as P

D = 1280
HD = 64
DL = 4096
KVH = 16
LHD = 128
MESH = pl.DeviceIdType.MESH
F32 = jnp.float32
BF16 = jnp.bfloat16


def place():
    mp, sec = lax.axis_index("mp"), lax.axis_index("section")
    return lax.axis_index("tm"), mp // 2, mp % 2, sec // 2, sec % 2


def device(y, x_hi, c, z, x_lo):
    return {"tm": y, "mp": x_hi * 2 + c, "section": z * 2 + x_lo}


def remote(src, dst, send, recv, target):
    return pltpu.make_async_remote_copy(
        src_ref=src, dst_ref=dst, send_sem=send, recv_sem=recv, device_id=target, device_id_type=MESH
    )


NEG = -1e30
TQ = 256
H0 = 32


def line(step, Z, Y):
    y, x_hi, c, z, x_lo = place()
    sections = 2 * Z
    at = lax.rem(y * sections + z * 2 + x_lo + step + Y * sections, Y * sections)
    return {"tm": at // sections, "mp": x_hi * 2 + c, "section": lax.rem(at, sections)}


def gelu(x):
    return 0.5 * x * (1.0 + lax.erf(x * math.sqrt(0.5)))


def greet(Z, Y):
    y, x_hi, c, z, x_lo = place()
    barrier = pltpu.get_barrier_semaphore()
    for step in (1, Z - 1):
        pl.semaphore_signal(
            barrier, inc=1, device_id=device(y, x_hi, c, lax.rem(z + step, Z), x_lo), device_id_type=MESH
        )
    for dy in range(Y):
        for k in range(8):
            if dy == 0 and k == 0:
                continue
            a, b, d = k // 4, (k // 2) % 2, k % 2
            other = device(
                lax.rem(y + dy, Y), lax.rem(x_hi + a, 2), lax.rem(c + b, 2), z, lax.rem(x_lo + d, 2)
            )
            pl.semaphore_signal(barrier, inc=1, device_id=other, device_id_type=MESH)
    pl.semaphore_signal(barrier, inc=1, device_id=line(jnp.where(x_lo == 1, 1, -1), Z, Y), device_id_type=MESH)
    pl.semaphore_wait(barrier, 8 * Y + 2)


class Across:
    def __init__(self, src, buf, send, recv):
        y, x_hi, c, z, x_lo = place()
        self.buf, self.send, self.recv, self.src = buf, send, recv, src
        self.me, self.twin, self.far, self.both = (
            x_hi * 2 + c, x_hi * 2 + 1 - c, (1 - x_hi) * 2 + c, (1 - x_hi) * 2 + 1 - c
        )
        self.to_twin = device(y, x_hi, 1 - c, z, x_lo)
        self.to_far = device(y, 1 - x_hi, c, z, x_lo)

    def copy(self, k, src, slot, target):
        return remote(src, self.buf.at[slot], self.send.at[k], self.recv.at[k], target)

    def start(self):
        self.copy(1, self.src, self.me, self.to_far).start()
        self.copy(0, self.src, self.me, self.to_twin).start()

    def relay(self):
        self.copy(1, self.buf.at[self.far], self.far, self.to_far).wait_recv()
        self.copy(2, self.buf.at[self.far], self.far, self.to_twin).start()

    def finish(self):
        self.copy(0, self.buf.at[self.twin], self.twin, self.to_twin).wait_recv()
        self.copy(2, self.buf.at[self.both], self.both, self.to_twin).wait_recv()
        for k in range(3):
            self.copy(k, self.buf.at[self.me], self.me, self.to_twin).wait_send()


class Sections:
    def __init__(self, src, buf, us, ur, ds, dr, ous, our, ods, odr, xs, xr, loc, h0):
        y, x_hi, c, z, x_lo = place()
        self.Z = buf.shape[0]
        self.src, self.buf, self.z, self.x = src, buf, z, x_lo
        self.s = (us, ur, ds, dr, ous, our, ods, odr, xs, xr)
        self.loc = loc
        self.lo = pl.ds(0, h0)
        self.hi = pl.ds(h0, src.shape[0] - h0)
        self.up = device(y, x_hi, c, lax.rem(z + 1, self.Z), x_lo)
        self.down = device(y, x_hi, c, lax.rem(z + self.Z - 1, self.Z), x_lo)
        self.side = device(y, x_hi, c, z, 1 - x_lo)

    def below(self, t):
        return lax.rem(self.z + self.Z - t, self.Z)

    def above(self, t):
        return lax.rem(self.z + t, self.Z)

    def ring(self, kind, t, zz, src=None):
        us, ur, ds, dr, ous, our, ods, odr, xs, xr = self.s
        if kind == "u":
            ref = self.buf.at[zz, self.x]
            return remote(ref if src is None else src, ref, us.at[t], ur.at[t], self.up)
        if kind == "d":
            ref = self.buf.at[zz, self.x]
            return remote(ref if src is None else src, ref, ds.at[t], dr.at[t], self.down)
        ref = self.buf.at[zz, 1 - self.x, self.lo]
        if kind == "ou":
            return remote(ref, ref, ous.at[t], our.at[t], self.up)
        return remote(ref, ref, ods.at[t], odr.at[t], self.down)

    def whole(self, x):
        us, ur, ds, dr, ous, our, ods, odr, xs, xr = self.s
        return remote(self.src, self.buf.at[self.z, x], xs.at[0], xr.at[0], self.side)

    def forward(self, k, zz, x):
        us, ur, ds, dr, ous, our, ods, odr, xs, xr = self.s
        ref = self.buf.at[zz, x, self.hi]
        return remote(ref, ref, xs.at[k], xr.at[k], self.side)

    def local(self):
        return pltpu.make_async_copy(self.src, self.buf.at[self.z, self.x], self.loc)

    def start(self):
        self.local().start()
        self.whole(self.x).start()
        self.ring("u", 0, self.z, self.src).start()
        self.ring("d", 0, self.z, self.src).start()

    def start_other(self):
        self.whole(1 - self.x).wait_recv()
        self.ring("ou", 0, self.z).start()
        self.ring("od", 0, self.z).start()

    def step(self, t):
        far = self.Z // 2
        zz = self.below(t)
        self.ring("u", t - 1, zz).wait_recv()
        if t < far:
            self.ring("u", t, zz).start()
        self.forward(2 * t - 1, zz, self.x).start()
        if t < far:
            zz = self.above(t)
            self.ring("d", t - 1, zz).wait_recv()
            if t < far - 1:
                self.ring("d", t, zz).start()
            self.forward(2 * t, zz, self.x).start()
        self.step_other(t)

    def step_other(self, t):
        far = self.Z // 2
        zz = self.below(t)
        self.ring("ou", t - 1, zz).wait_recv()
        if t < far:
            self.ring("ou", t, zz).start()
            zz = self.above(t)
            self.ring("od", t - 1, zz).wait_recv()
            if t < far - 1:
                self.ring("od", t, zz).start()

    def finish(self):
        far = self.Z // 2
        for t in range(1, far + 1):
            self.forward(2 * t - 1, self.below(t), 1 - self.x).wait_recv()
            if t < far:
                self.forward(2 * t, self.above(t), 1 - self.x).wait_recv()
        self.local().wait()
        self.whole(self.x).wait_send()
        for t in range(far):
            self.ring("u", t, self.z).wait_send()
            self.ring("ou", t, self.z).wait_send()
        for t in range(far - 1):
            self.ring("d", t, self.z).wait_send()
            self.ring("od", t, self.z).wait_send()
        for k in range(1, 2 * far):
            self.forward(k, self.z, self.x).wait_send()


class Quarters:
    def __init__(self, src, buf, us, ur, ds, dr, xs, xr, yus, yur, yds, ydr, rus, rur, rds, rdr, loc):
        y, x_hi, c, z, x_lo = place()
        self.Z, self.Y = buf.shape[0], buf.shape[2]
        self.src, self.buf, self.z, self.x, self.y = src, buf, z, x_lo, y
        self.s = (us, ur, ds, dr, xs, xr, yus, yur, yds, ydr, rus, rur, rds, rdr)
        self.loc = loc
        self.up = device(y, x_hi, c, lax.rem(z + 1, self.Z), x_lo)
        self.down = device(y, x_hi, c, lax.rem(z + self.Z - 1, self.Z), x_lo)
        self.side = device(y, x_hi, c, z, 1 - x_lo)
        self.yn, self.yp = lax.rem(y + 1, self.Y), lax.rem(y + self.Y - 1, self.Y)
        self.yf = lax.rem(y + 2, self.Y)
        self.next = device(self.yn, x_hi, c, z, x_lo)
        self.prev = device(self.yp, x_hi, c, z, x_lo)

    def zs(self, k):
        if k % 2:
            return lax.rem(self.z + self.Z - (k + 1) // 2, self.Z)
        return lax.rem(self.z + k // 2, self.Z)

    def ring(self, kind, t, zz):
        us, ur, ds, dr = self.s[:4]
        ref = self.buf.at[zz, :, self.y]
        if kind == "u":
            return remote(ref, ref, us.at[t], ur.at[t], self.up)
        return remote(ref, ref, ds.at[t], dr.at[t], self.down)

    def cross(self, x):
        xs, xr = self.s[4:6]
        return remote(self.src.at[self.y], self.buf.at[self.z, x, self.y], xs.at[0], xr.at[0], self.side)

    def local(self):
        return pltpu.make_async_copy(self.src, self.buf.at[self.z, self.x], self.loc)

    def spread(self, kind, k, quarter):
        yus, yur, yds, ydr = self.s[6:10]
        if k == 0:
            ref = self.buf.at[self.z, 1 - self.x, quarter]
        else:
            ref = self.buf.at[self.zs(k), :, quarter]
        if kind == "n":
            return remote(ref, ref, yus.at[k], yur.at[k], self.next)
        return remote(ref, ref, yds.at[k], ydr.at[k], self.prev)

    def relay(self, kind, k, quarter):
        rus, rur, rds, rdr = self.s[10:14]
        if kind == "n":
            ref = self.buf.at[self.zs(k), (1 - self.x) if k == 0 else 0, quarter]
            return remote(ref, ref, rus.at[k], rur.at[k], self.next)
        ref = self.buf.at[self.zs(k), 1, quarter]
        return remote(ref, ref, rds.at[k], rdr.at[k], self.prev)

    def start(self):
        self.cross(self.x).start()
        self.local().start()

    def begin(self):
        self.local().wait()
        self.cross(1 - self.x).wait_recv()
        self.spread("n", 0, self.y).start()
        self.spread("p", 0, self.y).start()
        self.ring("u", 0, self.z).start()
        self.ring("d", 0, self.z).start()

    def arrive(self, k):
        far, t, zz = self.Z // 2, (k + 1) // 2, self.zs(k)
        kind = "u" if k % 2 else "d"
        self.ring(kind, t - 1, zz).wait_recv()
        if t < (far if kind == "u" else far - 1):
            self.ring(kind, t, zz).start()
        self.spread("n", k, self.y).start()
        self.spread("p", k, self.y).start()

    def pass_on(self, k):
        self.spread("n", k, self.yp).wait_recv()
        self.relay("n", k, self.yp).start()
        self.spread("p", k, self.yn).wait_recv()
        if k:
            self.relay("p", k, self.yn).start()

    def finish(self):
        far = self.Z // 2
        for k in range(2 * far):
            self.relay("n", k, self.yf).wait_recv()
            if k:
                self.relay("p", k, self.yf).wait_recv()
        self.cross(self.x).wait_send()
        for t in range(far):
            self.ring("u", t, self.z).wait_send()
        for t in range(far - 1):
            self.ring("d", t, self.z).wait_send()
        for k in range(2 * far):
            self.spread("n", k, self.y).wait_send()
            self.spread("p", k, self.y).wait_send()
            self.relay("n", k, self.y).wait_send()
            if k:
                self.relay("p", k, self.y).wait_send()


def normal(rows, gain):
    center = jnp.mean(rows, axis=-1, keepdims=True)
    spread = jnp.mean(jnp.square(rows - center), axis=-1, keepdims=True)
    return (rows - center) * lax.rsqrt(spread + 1e-05) * gain


def layer_kernel(
    mel, w1, c2, gn, qw, ow, pw, kw, rg, cs, sn, out,
    hprev, hnext, w1f, gf, c2f, qwf, xe, even, odd, hbox, nbuf, pk,
    kv, qbox, qs, m, l, acc, obuf, abox, att, res, owf, pwf, kwf, pbox, sbox, keep, tsend, trecv, csend, crecv,
    kv_s, kv_r, q_s, q_r, loc, up_s, up_r, dn_s, dn_r, co_s, co_r, a_s, a_r,
    ow_s, ow_r, pb_s, pb_r, sb_s, sb_r, t_s, t_r, c_s, c_r,
    h_s, h_r, w1_s, w1_r, g_s, g_r, hb_s, hb_r,
    *rings,
):
    y, x_hi, c, z, x_lo = place()
    Z = kv.shape[0]
    n = qbox.shape[0]
    me = x_hi * 2 + c
    up = device(y, x_hi, c, lax.rem(z + 1, Z), x_lo)
    down = device(y, x_hi, c, lax.rem(z + Z - 1, Z), x_lo)
    twin = device(y, x_hi, 1 - c, z, x_lo)
    far_dev = device(y, 1 - x_hi, c, z, x_lo)
    peers = [device(i, x_hi, x_lo, z, c) for i in range(n)]
    mirror = c == x_lo

    outw = Across(ow, owf, ow_s, ow_r)
    proj = Sections(pw, pwf, *rings[0:10], loc.at[3], H0)
    conv = Sections(c2, c2f, *rings[10:20], loc.at[6], 96)
    qkv = Sections(qw, qwf, *rings[20:30], loc.at[7], H0)
    kvw = Quarters(kw, kwf, *rings[30:44], loc.at[4])
    first_w = Across(w1, w1f, w1_s, w1_r)
    gains = Across(gn, gf, g_s, g_r)
    own_w1 = pltpu.make_async_copy(w1, w1f.at[me], loc.at[8])
    own_g = pltpu.make_async_copy(gn, gf.at[me], loc.at[9])
    own_w1.start()
    own_g.start()
    count = mel.shape[0]
    greet(Z, n)

    tail16, head16 = pl.ds(count - 16, 16), pl.ds(0, 16)
    edge_next = remote(mel.at[tail16], hprev, h_s.at[0], h_r.at[0], line(1, Z, n))
    edge_prev = remote(mel.at[head16], hnext, h_s.at[1], h_r.at[1], line(-1, Z, n))
    first_w.start()
    edge_next.start()
    edge_prev.start()
    conv.start()
    gains.start()
    conv.start_other()
    first_w.relay()
    gains.relay()
    edge_next.wait_recv()
    edge_prev.wait_recv()
    block_at = y * 2 * Z + z * 2 + x_lo
    begins = jnp.where(block_at == 0, 0.0, 1.0)
    ends = jnp.where(block_at == 2 * Z * n - 1, 0.0, 1.0)
    xe[0:16, :] = hprev[...].astype(F32) * begins
    xe[16 : 16 + count, :] = mel[...].astype(F32)
    xe[16 + count :, :] = hnext[...].astype(F32) * ends
    left = jnp.concatenate(
        [xe[15 : 15 + count, 128:256], xe[16 : 16 + count, :]], axis=1
    ).astype(BF16)
    right = jnp.concatenate([xe[0 : 16 + count, :], xe[1 : 17 + count, 0:128]], axis=1).astype(BF16)
    inside = jnp.where(
        lax.broadcasted_iota(jnp.int32, (16 + count, 1), 0) >= 16, jnp.ones((16 + count, 1), F32), begins
    )
    own_w1.wait()
    first_w.finish()
    for part in range(4):
        even[part] = gelu(jnp.dot(left, w1f[part], preferred_element_type=F32)).astype(BF16)
        odd[part] = gelu(jnp.dot(right, w1f[part], preferred_element_type=F32)) * inside
        if part == 1:
            conv.step(1)
    conv.step(2)
    qkv.start()
    conv.step(3)
    qkv.start_other()
    conv.step(Z // 2)
    kvw.start()
    own_w = pltpu.make_async_copy(ow, owf.at[me], loc.at[5])
    own_w.start()
    conv.finish()

    rows2 = c2.shape[0] // 3
    wide = w1.shape[1]
    second = jnp.zeros((count, wide), F32)
    for part in range(4):
        taps = (
            odd[part, 15 : 15 + count, :].astype(BF16),
            even[part],
            odd[part, 16 : 16 + count, :].astype(BF16),
        )
        for tap in range(3):
            w = c2f[2 * part : 2 * part + 2, :, tap * rows2 : (tap + 1) * rows2, :].reshape(4 * rows2, wide)
            second = second + jnp.dot(taps[tap], w, preferred_element_type=F32)
    hbox[me] = gelu(second).astype(BF16)
    share_h = Across(hbox.at[me], hbox, hb_s, hb_r)
    share_h.start()
    qkv.step(1)
    share_h.relay()
    qkv.step(2)
    own_g.wait()
    gains.finish()
    share_h.finish()
    parts = [hbox[k].astype(F32) for k in range(4)]
    center = sum(jnp.sum(p, axis=1, keepdims=True) for p in parts) / D
    parts = [p - center for p in parts]
    inv = lax.rsqrt(sum(jnp.sum(p * p, axis=1, keepdims=True) for p in parts) / D + 1e-05)
    for k in range(4):
        nbuf[k] = (parts[k] * inv * gf[k, 0:1, :]).astype(BF16)
    qkv.step(3)
    kvw.begin()
    qkv.step(Z // 2)
    qkv.finish()
    projected = jnp.zeros((count, qw.shape[1]), F32)
    for k in range(4):
        projected = projected + jnp.dot(
            nbuf[k], qwf[2 * k : 2 * k + 2].reshape(4 * qw.shape[0], qw.shape[1]), preferred_element_type=F32
        )
    split = count // 2
    lower = lax.broadcasted_iota(jnp.int32, (split, 128), 1) < HD
    for i in range(n):
        pk[i, 0:count, :] = projected[:, i * 128 : (i + 1) * 128].astype(BF16)
        at = n * 128 + (i // 2) * 128
        a, b = projected[0:split, at : at + 128], projected[split:, at : at + 128]
        if i % 2 == 0:
            mixed_q = jnp.where(lower, a, pltpu.roll(b, HD, 1))
        else:
            mixed_q = jnp.where(lower, pltpu.roll(a, HD, 1), b)
        pk[i, count:, :] = mixed_q.astype(BF16)

    half = kv.shape[2] // n
    for i in range(n):
        own = jnp.logical_and(mirror, y == i)
        rows = pl.ds(pl.multiple_of(y * half, half), half)

        @pl.when(jnp.logical_not(own))
        def _():
            remote(pk.at[i, 0:half], kv.at[z, x_lo, rows], kv_s.at[i], kv_r.at[y], peers[i]).start()
            remote(pk.at[i, half:], qbox.at[y], q_s.at[i], q_r.at[y], peers[i]).start()

        @pl.when(own)
        def _():
            pltpu.make_async_copy(pk.at[i, 0:half], kv.at[z, c, rows], loc.at[0]).start()
            pltpu.make_async_copy(pk.at[i, half:], qbox.at[y], loc.at[1]).start()

    m[...] = jnp.full(m.shape, NEG, F32)
    l[...] = jnp.zeros(l.shape, F32)
    acc[...] = jnp.zeros(acc.shape, F32)

    for i in range(n):
        own = jnp.logical_and(mirror, y == i)
        rows = pl.ds(i * half, half)

        @pl.when(jnp.logical_not(own))
        def _():
            remote(pk.at[i, 0:half], kv.at[z, c, rows], kv_s.at[i], kv_r.at[i], peers[i]).wait()
            remote(pk.at[i, half:], qbox.at[i], q_s.at[i], q_r.at[i], peers[i]).wait()

        @pl.when(own)
        def _():
            pltpu.make_async_copy(pk.at[i, 0:half], kv.at[z, c, rows], loc.at[0]).wait()
            pltpu.make_async_copy(pk.at[i, half:], qbox.at[i], loc.at[1]).wait()

    def block(ref_z, core):
        return kv.at[ref_z, core]

    def send_up(t, zz):
        return remote(block(zz, c), block(zz, c), up_s.at[t], up_r.at[t], up)

    def send_down(t, zz):
        return remote(block(zz, c), block(zz, c), dn_s.at[t], dn_r.at[t], down)

    def share(k, zz):
        return remote(block(zz, c), block(zz, c), co_s.at[k], co_r.at[k], twin)

    def taken(k, zz):
        return remote(block(zz, 1 - c), block(zz, 1 - c), co_s.at[k], co_r.at[k], twin)

    send_up(0, z).start()
    send_down(0, z).start()
    share(0, z).start()
    outw.start()

    lanes = lax.broadcasted_iota(jnp.int32, (half // 2, 128), 1)
    for i in range(n):
        raw = qbox[i].astype(F32) * 0.125
        qs[i * half : i * half + half // 2, :] = jnp.where(lanes < HD, raw, 0.0).astype(BF16)
        qs[i * half + half // 2 : (i + 1) * half, :] = jnp.where(
            lanes < HD, pltpu.roll(raw, HD, 1), 0.0
        ).astype(BF16)

    total = qs.shape[0]
    width = kv.shape[2]

    def process(zz, core):
        def tile(k, carry):
            rows = pl.ds(pl.multiple_of(k * TQ, TQ), TQ)
            pairs = kv[zz, core]
            s = lax.dot_general(
                qs[rows, :], pairs, (((1,), (1,)), ((), ())), preferred_element_type=F32
            )
            old = m[rows, :]
            new = jnp.maximum(old, jnp.max(s, axis=1, keepdims=True))
            m[rows, :] = new
            decay = jnp.exp(old - new)
            w = jnp.exp(s - jnp.concatenate([new] * (width // 128), axis=1))
            part = w[:, 0:128]
            for piece in range(1, width // 128):
                part = part + w[:, piece * 128 : (piece + 1) * 128]
            l[rows, :] = l[rows, :] * decay + part
            acc[rows, :] = acc[rows, :] * decay + jnp.dot(
                w.astype(BF16), pairs, preferred_element_type=F32
            )
            return carry

        lax.fori_loop(0, total // TQ, tile, 0)

    process(z, c)
    taken(0, z).wait_recv()
    process(z, 1 - c)
    far = Z // 2
    kvw.pass_on(0)
    for t in range(1, far + 1):
        below = lax.rem(z + Z - t, Z)
        above = lax.rem(z + t, Z)
        send_up(t - 1, below).wait_recv()
        if t < far:
            send_up(t, below).start()
        share(2 * t - 1, below).start()
        if t < far:
            send_down(t - 1, above).wait_recv()
            if t < far - 1:
                send_down(t, above).start()
            share(2 * t, above).start()
        process(below, c)
        kvw.arrive(2 * t - 1)
        if t < far:
            kvw.arrive(2 * t)
        if t > 1:
            kvw.pass_on(2 * t - 3)
            kvw.pass_on(2 * t - 2)
        if t < far:
            process(above, c)
        if t == 1:
            proj.start()
        taken(2 * t - 1, below).wait_recv()
        process(below, 1 - c)
        if t == 2:
            proj.start_other()
            outw.relay()
        if t == 3:
            proj.step(1)
        if t < far:
            taken(2 * t, above).wait_recv()
            process(above, 1 - c)
        if t == 3:
            proj.step(2)
        if t == 4:
            proj.step(3)

    quarter = half // 4
    low = lax.broadcasted_iota(jnp.int32, (quarter // 2, 128), 1) < HD
    head = (x_hi * 2 + x_lo) * n + y

    def give(j, q, slot, sem):
        k = 4 * j + q
        return remote(obuf.at[k], abox.at[slot], a_s.at[k], a_r.at[sem], device(j, q // 2, q % 2, z, c))

    for j in range(n):
        for q in range(4):
            k = 4 * j + q
            at = j * half + q * quarter
            top, bot = pl.ds(at, quarter // 2), pl.ds(at + quarter // 2, quarter // 2)
            first = pltpu.roll(acc[top, :] / jnp.sum(l[top, :], axis=1, keepdims=True), HD, 1)
            second = acc[bot, :] / jnp.sum(l[bot, :], axis=1, keepdims=True)
            obuf[k] = jnp.where(low, first, second).astype(BF16)
    for j in range(n):
        for q in range(4):
            own = jnp.logical_and(mirror, jnp.logical_and(y == j, me == q))

            @pl.when(jnp.logical_not(own))
            def _():
                give(j, q, head, head).start()

            @pl.when(own)
            def _():
                pltpu.make_async_copy(obuf.at[4 * j + q], abox.at[head], loc.at[0]).start()

    proj.step(far)
    kvw.pass_on(2 * far - 1)

    for t in range(far):
        send_up(t, z).wait_send()
    for t in range(far - 1):
        send_down(t, z).wait_send()
    for k in range(2 * far):
        share(k, z).wait_send()
    outw.finish()
    own_w.wait()

    for h in range(4 * n):
        own = jnp.logical_and(mirror, head == h)

        @pl.when(jnp.logical_not(own))
        def _():
            remote(obuf.at[h], abox.at[h], a_s.at[h], a_r.at[h], twin).wait_recv()

        @pl.when(own)
        def _():
            pltpu.make_async_copy(obuf.at[h], abox.at[h], loc.at[0]).wait()

    for pair in range(2 * n):
        a = abox[2 * pair].astype(F32)
        b = abox[2 * pair + 1].astype(F32)
        cols = slice(pair * 128, (pair + 1) * 128)
        att[0 : quarter // 2, cols] = jnp.where(low, a, pltpu.roll(b, HD, 1)).astype(BF16)
        att[quarter // 2 :, cols] = jnp.where(low, pltpu.roll(a, HD, 1), b).astype(BF16)

    mixed = jnp.dot(
        att[...], owf[...].reshape(4 * ow.shape[0], ow.shape[1]), preferred_element_type=F32
    )
    tokens = quarter // 2
    pieces = []
    mine = pl.ds(pl.multiple_of(me * quarter, quarter), quarter)
    own_rows = jnp.concatenate([hbox[k, mine, :].astype(F32) for k in range(4)], axis=1)
    gain = jnp.concatenate([gf[k, 1:2, :] for k in range(4)], axis=1)
    for k in range(D // 128):
        at = slice(k * 128, (k + 1) * 128)
        res[k] = own_rows[:, at] + mixed[:, at]
        pieces.append(
            (res.at[k][pl.ds(0, tokens, stride=2), :] + res.at[k][pl.ds(1, tokens, stride=2), :]) * 0.5
        )
    pooled = jnp.concatenate(pieces, axis=1)
    pbox[me] = normal(pooled, gain).astype(BF16)
    gather = Across(pbox.at[me], pbox, pb_s, pb_r)
    gather.start()
    gather.relay()
    proj.finish()
    gather.finish()

    post = pbox[...].reshape(4 * tokens, pbox.shape[2])
    embedded = jnp.dot(
        post, pwf[...].reshape(2 * Z * pw.shape[0], pw.shape[1]), preferred_element_type=F32
    ).astype(BF16)
    widened = embedded.astype(F32)
    sbox[me] = jnp.broadcast_to(
        jnp.sum(widened * widened, axis=1, keepdims=True), (4 * tokens, 128)
    )
    squares = Across(sbox.at[me], sbox, sb_s, sb_r)
    squares.start()
    gained = (widened * rg[0:1, :]).astype(BF16)
    cols = pw.shape[1]
    kvw.finish()

    def columns(a, b):
        at = pl.ds(pl.multiple_of((a * 2 + b) * cols, cols), cols)
        return jnp.dot(
            gained, kwf[:, :, :, :, at].reshape(cols, cols), preferred_element_type=F32
        )

    def swap(k):
        return remote(tsend.at[k], trecv.at[k], t_s.at[k], t_r.at[k], twin)

    over = remote(csend, crecv, c_s.at[0], c_r.at[0], far_dev)
    tsend[0] = columns(1 - x_hi, 1 - c).astype(BF16)
    swap(0).start()
    keep[...] = columns(1 - x_hi, c)
    squares.relay()
    swap(0).wait_recv()
    csend[...] = (keep[...] + trecv[0].astype(F32)).astype(BF16)
    over.start()
    tsend[1] = columns(x_hi, 1 - c).astype(BF16)
    swap(1).start()
    keep[...] = columns(x_hi, c)
    squares.finish()
    scale = lax.rsqrt((sbox[0] + sbox[1] + sbox[2] + sbox[3]) / DL + 1e-06)
    swap(1).wait_recv()
    keep[...] = keep[...] + trecv[1].astype(F32)
    over.wait_recv()
    for h in range(cols // LHD):
        at = slice(h * LHD, (h + 1) * LHD)
        value = (keep[:, at] + crecv[:, at].astype(F32)) * scale
        out[:, at] = (value * cs[...] + pltpu.roll(value, HD, 1) * sn[...]).astype(BF16)

    edge_next.wait_send()
    edge_prev.wait_send()
    swap(0).wait_send()
    swap(1).wait_send()
    over.wait_send()
    for j in range(n):
        for q in range(4):
            own = jnp.logical_and(mirror, jnp.logical_and(y == j, me == q))

            @pl.when(jnp.logical_not(own))
            def _():
                give(j, q, head, head).wait_send()


def layer(mel, w1, c2, gn, qw, ow, pw, kw, rg, cs, sn):
    frames = mel.shape[0]
    n = lax.axis_size("tm")
    Z = lax.axis_size("section") // 2
    total = frames * n
    tokens = frames // 2
    quarter = frames // 4
    cols = pw.shape[1]
    wide = w1.shape[1]
    sem = pltpu.SemaphoreType.DMA
    vm = pl.BlockSpec(memory_space=pltpu.VMEM)
    V = pltpu.VMEM
    half = Z // 2
    ring = [sem((half,))] * 8 + [sem((Z,))] * 2
    return pl.pallas_call(
        layer_kernel,
        out_shape=jax.ShapeDtypeStruct((tokens, cols), BF16),
        in_specs=[vm] * 11,
        out_specs=vm,
        scratch_shapes=[
            V((16, mel.shape[1]), BF16),
            V((16, mel.shape[1]), BF16),
            V((4,) + w1.shape, BF16),
            V((4,) + gn.shape, F32),
            V((Z, 2) + c2.shape, BF16),
            V((Z, 2) + qw.shape, BF16),
            V((frames + 32, mel.shape[1]), F32),
            V((4, frames, wide), BF16),
            V((4, frames + 16, wide), F32),
            V((4, frames, wide), BF16),
            V((4, frames, wide), BF16),
            V((n, frames + tokens, 128), BF16),
            V((Z, 2, total, 128), BF16),
            V((n, tokens, 128), BF16),
            V((total, 128), BF16),
            V((total, 128), F32),
            V((total, 128), F32),
            V((total, 128), F32),
            V((16, quarter // 2, 128), BF16),
            V((16, quarter // 2, 128), BF16),
            V((quarter, ow.shape[0] * 4), BF16),
            V((ow.shape[1] // 128, quarter, 128), F32),
            V((4,) + ow.shape, BF16),
            V((Z, 2) + pw.shape, BF16),
            V((Z, 2) + kw.shape, BF16),
            V((4, quarter // 2, ow.shape[1]), BF16),
            V((4, tokens, 128), F32),
            V((tokens, cols), F32),
            V((2, tokens, cols), BF16),
            V((2, tokens, cols), BF16),
            V((tokens, cols), BF16),
            V((tokens, cols), BF16),
            sem((n,)), sem((n,)), sem((n,)), sem((n,)), sem((10,)),
            sem((half,)), sem((half,)), sem((half,)), sem((half,)), sem((Z,)), sem((Z,)), sem((16,)), sem((16,)),
            sem((3,)), sem((3,)), sem((3,)), sem((3,)), sem((3,)), sem((3,)), sem((2,)), sem((2,)), sem((1,)), sem((1,)),
            sem((2,)), sem((2,)), sem((3,)), sem((3,)), sem((3,)), sem((3,)), sem((3,)), sem((3,)),
        ]
        + ring * 3
        + [sem((half,))] * 4 + [sem((1,))] * 2 + [sem((Z,))] * 8,
        compiler_params=pltpu.CompilerParams(
            collective_id=1, has_side_effects=True, vmem_limit_bytes=60 * 2**20
        ),
    )(mel, w1, c2, gn, qw, ow, pw, kw, rg, cs, sn)


def tables(rows, cols):
    row_start = (lax.axis_index("tm") * lax.axis_size("section") + lax.axis_index("section")) * rows
    positions = (row_start + jnp.arange(rows, dtype=jnp.int32)).astype(F32)
    within = jnp.arange(LHD, dtype=jnp.int32)
    freq = jnp.power(10000.0, -2.0 * (within % (LHD // 2)).astype(F32) / LHD)
    angle = positions[:, None] * freq[None, :]
    keys = lax.axis_index("mp") * cols < KVH * LHD
    sines = jnp.where(within < LHD // 2, -1.0, 1.0) * jnp.sin(angle)
    return jnp.where(keys, jnp.cos(angle), 1.0), jnp.where(keys, sines, 0.0)


def shards(
    mel_frames,
    conv1_weight,
    conv2_weight,
    attn_gain,
    qkv_weight,
    out_weight,
    post_gain,
    proj_weight,
    rms_gain,
    kv_weight,
):
    frames = mel_frames.shape[0] // 2
    bins, wide = conv1_weight.shape[1:]
    rows, _, width = qkv_weight.shape
    heads = width // HD
    split = qkv_weight.reshape(rows, 3, heads, HD)
    pairs = jnp.stack([split[:, 1], split[:, 2]], axis=2).reshape(rows, 2 * width)
    weight = jnp.concatenate([pairs, qkv_weight[:, 0]], axis=1)
    gains = jnp.pad(jnp.stack([attn_gain, post_gain]), ((0, 6), (0, 0)))
    cs, sn = tables(frames // 2, proj_weight.shape[1])
    return layer(
        mel_frames.reshape(frames, 2 * bins),
        conv1_weight.reshape(3 * bins, wide),
        conv2_weight.reshape(-1, wide),
        gains,
        weight,
        out_weight,
        proj_weight,
        kv_weight.reshape(4, kv_weight.shape[0] // 4, kv_weight.shape[1]),
        rms_gain.reshape(1, -1),
        cs,
        sn,
    )


def solution(mesh):
    return jax.shard_map(
        shards,
        mesh=mesh,
        in_specs=(
            P(("tm", "section"), None),
            P(None, None, "mp"),
            P(None, "section", "mp"),
            P("mp"),
            P("section", None, "mp"),
            P("mp", None),
            P("mp"),
            P("section", "mp"),
            P("mp"),
            P(("mp", "section"), None),
        ),
        out_specs=P(("tm", "section"), "mp"),
        check_vma=False,
    )
```

```python
import functools
import math

import jax
import jax.numpy as jnp
from jax import lax
from jax.experimental import pallas as pl
from jax.experimental.pallas import tpu as pltpu
from jax.sharding import PartitionSpec as P

D = 1280
HD = 64
DL = 4096
KVH = 16
LHD = 128
MESH = pl.DeviceIdType.MESH
F32 = jnp.float32
BF16 = jnp.bfloat16


def place():
    mp, sec = lax.axis_index("mp"), lax.axis_index("section")
    return lax.axis_index("tm"), mp // 2, mp % 2, sec // 2, sec % 2


def device(y, x_hi, c, z, x_lo):
    return {"tm": y, "mp": x_hi * 2 + c, "section": z * 2 + x_lo}


def remote(src, dst, send, recv, target):
    return pltpu.make_async_remote_copy(
        src_ref=src, dst_ref=dst, send_sem=send, recv_sem=recv, device_id=target, device_id_type=MESH
    )


NEG = -1e30
BY_Y = 128
ROWS_Y = 64


def line(step, Z, Y):
    y, x_hi, c, z, x_lo = place()
    sections = 2 * Z
    at = lax.rem(y * sections + z * 2 + x_lo + step + Y * sections, Y * sections)
    return {"tm": at // sections, "mp": x_hi * 2 + c, "section": lax.rem(at, sections)}


def gelu(x):
    return 0.5 * x * (1.0 + lax.erf(x * math.sqrt(0.5)))


def greet(Z, Y):
    y, x_hi, c, z, x_lo = place()
    barrier = pltpu.get_barrier_semaphore()
    for step in (1, Z - 1):
        pl.semaphore_signal(
            barrier, inc=1, device_id=device(y, x_hi, c, lax.rem(z + step, Z), x_lo), device_id_type=MESH
        )
    for dy in range(Y):
        for k in range(8):
            if dy == 0 and k == 0:
                continue
            a, b, d = k // 4, (k // 2) % 2, k % 2
            other = device(
                lax.rem(y + dy, Y), lax.rem(x_hi + a, 2), lax.rem(c + b, 2), z, lax.rem(x_lo + d, 2)
            )
            pl.semaphore_signal(barrier, inc=1, device_id=other, device_id_type=MESH)
    pl.semaphore_signal(barrier, inc=1, device_id=line(jnp.where(x_lo == 1, 1, -1), Z, Y), device_id_type=MESH)
    pl.semaphore_wait(barrier, 8 * Y + 2)


class Across:
    def __init__(self, src, buf, send, recv, near=False):
        y, x_hi, c, z, x_lo = place()
        self.buf, self.send, self.recv, self.src = buf, send, recv, src
        self.me, self.twin, self.far, self.both = (
            x_hi * 2 + c, x_hi * 2 + 1 - c, (1 - x_hi) * 2 + c, (1 - x_hi) * 2 + 1 - c
        )
        self.to_twin = device(y, x_hi, 1 - c, z, x_lo)
        self.to_far = device(y, 1 - x_hi, c, z, 1 - x_lo if near else x_lo)

    def copy(self, k, src, slot, target):
        return remote(src, self.buf.at[slot], self.send.at[k], self.recv.at[k], target)

    def start(self):
        self.copy(1, self.src, self.me, self.to_far).start()
        self.copy(0, self.src, self.me, self.to_twin).start()

    def relay(self):
        self.copy(1, self.buf.at[self.far], self.far, self.to_far).wait_recv()
        self.copy(2, self.buf.at[self.far], self.far, self.to_twin).start()

    def finish(self):
        self.copy(0, self.buf.at[self.twin], self.twin, self.to_twin).wait_recv()
        self.copy(2, self.buf.at[self.both], self.both, self.to_twin).wait_recv()
        for k in range(3):
            self.copy(k, self.buf.at[self.me], self.me, self.to_twin).wait_send()


class Sections:
    def __init__(self, src, buf, us, ur, ds, dr, ous, our, ods, odr, xs, xr, loc, h0):
        y, x_hi, c, z, x_lo = place()
        self.Z = buf.shape[0]
        self.src, self.buf, self.z, self.x = src, buf, z, x_lo
        self.s = (us, ur, ds, dr, ous, our, ods, odr, xs, xr)
        self.loc = loc
        self.lo = pl.ds(0, h0)
        self.hi = pl.ds(h0, src.shape[0] - h0)
        self.up = device(y, x_hi, c, lax.rem(z + 1, self.Z), x_lo)
        self.down = device(y, x_hi, c, lax.rem(z + self.Z - 1, self.Z), x_lo)
        self.side = device(y, x_hi, c, z, 1 - x_lo)

    def below(self, t):
        return lax.rem(self.z + self.Z - t, self.Z)

    def above(self, t):
        return lax.rem(self.z + t, self.Z)

    def ring(self, kind, t, zz, src=None):
        us, ur, ds, dr, ous, our, ods, odr, xs, xr = self.s
        if kind == "u":
            ref = self.buf.at[zz, self.x]
            return remote(ref if src is None else src, ref, us.at[t], ur.at[t], self.up)
        if kind == "d":
            ref = self.buf.at[zz, self.x]
            return remote(ref if src is None else src, ref, ds.at[t], dr.at[t], self.down)
        ref = self.buf.at[zz, 1 - self.x, self.lo]
        if kind == "ou":
            return remote(ref, ref, ous.at[t], our.at[t], self.up)
        return remote(ref, ref, ods.at[t], odr.at[t], self.down)

    def whole(self, x):
        us, ur, ds, dr, ous, our, ods, odr, xs, xr = self.s
        return remote(self.src, self.buf.at[self.z, x], xs.at[0], xr.at[0], self.side)

    def forward(self, k, zz, x):
        us, ur, ds, dr, ous, our, ods, odr, xs, xr = self.s
        ref = self.buf.at[zz, x, self.hi]
        return remote(ref, ref, xs.at[k], xr.at[k], self.side)

    def local(self):
        return pltpu.make_async_copy(self.src, self.buf.at[self.z, self.x], self.loc)

    def start(self):
        self.local().start()
        self.whole(self.x).start()
        self.ring("u", 0, self.z, self.src).start()
        self.ring("d", 0, self.z, self.src).start()

    def start_other(self):
        self.whole(1 - self.x).wait_recv()
        self.ring("ou", 0, self.z).start()
        self.ring("od", 0, self.z).start()

    def step(self, t):
        far = self.Z // 2
        zz = self.below(t)
        self.ring("u", t - 1, zz).wait_recv()
        if t < far:
            self.ring("u", t, zz).start()
        self.forward(2 * t - 1, zz, self.x).start()
        if t < far:
            zz = self.above(t)
            self.ring("d", t - 1, zz).wait_recv()
            if t < far - 1:
                self.ring("d", t, zz).start()
            self.forward(2 * t, zz, self.x).start()
        self.step_other(t)

    def step_other(self, t):
        far = self.Z // 2
        zz = self.below(t)
        self.ring("ou", t - 1, zz).wait_recv()
        if t < far:
            self.ring("ou", t, zz).start()
            zz = self.above(t)
            self.ring("od", t - 1, zz).wait_recv()
            if t < far - 1:
                self.ring("od", t, zz).start()

    def finish(self):
        far = self.Z // 2
        for t in range(1, far + 1):
            self.forward(2 * t - 1, self.below(t), 1 - self.x).wait_recv()
            if t < far:
                self.forward(2 * t, self.above(t), 1 - self.x).wait_recv()
        self.local().wait()
        self.whole(self.x).wait_send()
        for t in range(far):
            self.ring("u", t, self.z).wait_send()
            self.ring("ou", t, self.z).wait_send()
        for t in range(far - 1):
            self.ring("d", t, self.z).wait_send()
            self.ring("od", t, self.z).wait_send()
        for k in range(1, 2 * far):
            self.forward(k, self.z, self.x).wait_send()


class Quarters:
    def __init__(self, src, buf, us, ur, ds, dr, xs, xr, yus, yur, yds, ydr, rus, rur, rds, rdr, loc, other=None, Y=4):
        y, x_hi, c, z, x_lo = place()
        self.Z, self.Y = buf.shape[0], Y
        self.rows = buf.shape[2] // Y
        self.other = src if other is None else other
        self.src, self.buf, self.z, self.x, self.y = src, buf, z, x_lo, y if Y > 1 else 0
        self.s = (us, ur, ds, dr, xs, xr, yus, yur, yds, ydr, rus, rur, rds, rdr)
        self.loc = loc
        self.up = device(y, x_hi, c, lax.rem(z + 1, self.Z), x_lo)
        self.down = device(y, x_hi, c, lax.rem(z + self.Z - 1, self.Z), x_lo)
        self.side = device(y, x_hi, c, z, 1 - x_lo)
        self.yn, self.yp, self.yf = lax.rem(y + 1, 4), lax.rem(y + 3, 4), lax.rem(y + 2, 4)
        self.next = device(self.yn, x_hi, c, z, x_lo)
        self.prev = device(self.yp, x_hi, c, z, x_lo)

    def part(self, q):
        if self.Y == 1:
            return pl.ds(0, self.rows)
        return pl.ds(pl.multiple_of(q * self.rows, self.rows), self.rows)

    def zs(self, k):
        if k % 2:
            return lax.rem(self.z + self.Z - (k + 1) // 2, self.Z)
        return lax.rem(self.z + k // 2, self.Z)

    def ring(self, kind, t, zz):
        us, ur, ds, dr = self.s[:4]
        ref = self.buf.at[zz, :, self.part(self.y)]
        if kind == "u":
            return remote(ref, ref, us.at[t], ur.at[t], self.up)
        return remote(ref, ref, ds.at[t], dr.at[t], self.down)

    def cross(self, x):
        xs, xr = self.s[4:6]
        at = self.part(self.y)
        return remote(self.other.at[at], self.buf.at[self.z, x, at], xs.at[0], xr.at[0], self.side)

    def local(self):
        return pltpu.make_async_copy(self.src, self.buf.at[self.z, self.x], self.loc)

    def spread(self, kind, k, quarter):
        yus, yur, yds, ydr = self.s[6:10]
        if k == 0:
            ref = self.buf.at[self.z, 1 - self.x, self.part(quarter)]
        else:
            ref = self.buf.at[self.zs(k), :, self.part(quarter)]
        if kind == "n":
            return remote(ref, ref, yus.at[k], yur.at[k], self.next)
        return remote(ref, ref, yds.at[k], ydr.at[k], self.prev)

    def relay(self, kind, k, quarter):
        rus, rur, rds, rdr = self.s[10:14]
        if kind == "n":
            ref = self.buf.at[self.zs(k), (1 - self.x) if k == 0 else 0, self.part(quarter)]
            return remote(ref, ref, rus.at[k], rur.at[k], self.next)
        ref = self.buf.at[self.zs(k), 1, self.part(quarter)]
        return remote(ref, ref, rds.at[k], rdr.at[k], self.prev)

    def start(self):
        self.cross(self.x).start()
        self.local().start()

    def begin(self):
        self.local().wait()
        self.cross(1 - self.x).wait_recv()
        self.ring("u", 0, self.z).start()
        self.ring("d", 0, self.z).start()
        if self.Y > 1:
            self.spread("n", 0, self.y).start()
            self.spread("p", 0, self.y).start()

    def fetch(self, k):
        self.ring("u" if k % 2 else "d", (k + 1) // 2 - 1, self.zs(k)).wait_recv()
        if self.Y > 1:
            self.spread("n", k, self.y).start()
            self.spread("p", k, self.y).start()

    def onward(self, k):
        far, t = self.Z // 2, (k + 1) // 2
        kind = "u" if k % 2 else "d"
        if t < (far if kind == "u" else far - 1):
            self.ring(kind, t, self.zs(k)).start()

    def arrive(self, k):
        self.fetch(k)
        self.onward(k)

    def pass_on(self, k):
        self.spread("n", k, self.yp).wait_recv()
        self.relay("n", k, self.yp).start()
        self.spread("p", k, self.yn).wait_recv()
        if k:
            self.relay("p", k, self.yn).start()

    def finish(self):
        far = self.Z // 2
        turns = range(2 * far if self.Y > 1 else 0)
        for k in turns:
            self.relay("n", k, self.yf).wait_recv()
            if k:
                self.relay("p", k, self.yf).wait_recv()
        self.cross(self.x).wait_send()
        for t in range(far):
            self.ring("u", t, self.z).wait_send()
        for t in range(far - 1):
            self.ring("d", t, self.z).wait_send()
        for k in turns:
            self.spread("n", k, self.y).wait_send()
            self.spread("p", k, self.y).wait_send()
            self.relay("n", k, self.y).wait_send()
            if k:
                self.relay("p", k, self.y).wait_send()


def normal(rows, gain):
    center = jnp.mean(rows, axis=-1, keepdims=True)
    spread = jnp.mean(jnp.square(rows - center), axis=-1, keepdims=True)
    return (rows - center) * lax.rsqrt(spread + 1e-05) * gain


def layer_kernel(
    mel, w1, c2, gn, qw, ow, pw, kw, rg, cs, sn, out,
    hprev, hnext, w1f, gf, c2f, c2y, qwy, qwz, kwa, xe, even, odd, hbox, nbuf, pk,
    kv, qbox, qs, m, l, acc, obuf, abox, att, res, owf, pwy, pwz, kwf, pbox, sbox, ebox, keep, tsend, trecv, csend, crecv, psend, precv,
    kv_s, kv_r, q_s, q_r, loc, up_s, up_r, dn_s, dn_r, co_s, co_r, a_s, a_r,
    ow_s, ow_r, pb_s, pb_r, sb_s, sb_r, t_s, t_r, c_s, c_r, e_s, e_r,
    h_s, h_r, w1_s, w1_r, g_s, g_r, hb_s, hb_r,
    *rings,
):
    y, x_hi, c, z, x_lo = place()
    Z = kv.shape[0]
    n = qbox.shape[0]
    me = x_hi * 2 + c
    up = device(y, x_hi, c, lax.rem(z + 1, Z), x_lo)
    down = device(y, x_hi, c, lax.rem(z + Z - 1, Z), x_lo)
    twin = device(y, x_hi, 1 - c, z, x_lo)
    far_dev = device(y, 1 - x_hi, c, z, x_lo)
    peers = [device(i, x_hi, x_lo, z, c) for i in range(n)]
    mirror = c == x_lo

    outw = Across(ow, owf, ow_s, ow_r, True)
    quarters, pairs = rings[10:66], rings[66:78]
    none = (None,) * 8
    proj_y = Quarters(pw.at[pl.ds(0, ROWS_Y)], pwy, *quarters[0:14], loc.at[3])
    proj_z = Quarters(pw.at[pl.ds(ROWS_Y, pw.shape[0] - ROWS_Y)], pwz, *pairs[0:6], *none, loc.at[10], Y=1)
    qkv_y = Quarters(qw.at[pl.ds(0, ROWS_Y)], qwy, *quarters[14:28], loc.at[7])
    qkv_z = Quarters(qw.at[pl.ds(ROWS_Y, qw.shape[0] - ROWS_Y)], qwz, *pairs[6:12], *none, loc.at[11], Y=1)
    conv = Sections(c2.at[pl.ds(BY_Y, c2.shape[0] - BY_Y)], c2f, *rings[0:10], loc.at[6], 48)
    conv_y = Quarters(c2.at[pl.ds(0, BY_Y)], c2y, *quarters[28:42], loc.at[2])
    kvw = Quarters(kwa.at[x_lo], kwf, *quarters[42:56], loc.at[4], kwa.at[1 - x_lo])
    first_w = Across(w1, w1f, w1_s, w1_r, True)
    gains = Across(gn, gf, g_s, g_r, True)
    own_w1 = pltpu.make_async_copy(w1, w1f.at[me], loc.at[8])
    own_g = pltpu.make_async_copy(gn, gf.at[me], loc.at[9])
    own_w1.start()
    own_g.start()
    wide_c = kw.shape[1] // 8
    arrange = [
        pltpu.make_async_copy(
            kw.at[:, pl.ds((2 * k + h) * wide_c, wide_c)], kwa.at[h, :, pl.ds(k * wide_c, wide_c)], loc.at[12 + 4 * h + k]
        )
        for h in range(2)
        for k in range(4)
    ]
    for copy in arrange:
        copy.start()
    count = mel.shape[0]
    greet(Z, n)

    tail16, head16 = pl.ds(count - 16, 16), pl.ds(0, 16)
    edge_next = remote(mel.at[tail16], hprev, h_s.at[0], h_r.at[0], line(1, Z, n))
    edge_prev = remote(mel.at[head16], hnext, h_s.at[1], h_r.at[1], line(-1, Z, n))
    conv_y.start()
    conv.start()
    first_w.start()
    edge_next.start()
    edge_prev.start()
    gains.start()
    qkv_y.start()
    qkv_z.start()
    conv_y.begin()
    conv.start_other()
    qkv_y.begin()
    qkv_z.begin()
    first_w.relay()
    gains.relay()
    for copy in arrange:
        copy.wait()
    kvw.start()
    proj_y.start()
    proj_z.start()
    own_w = pltpu.make_async_copy(ow, owf.at[me], loc.at[5])
    own_w.start()
    edge_next.wait_recv()
    edge_prev.wait_recv()
    block_at = y * 2 * Z + z * 2 + x_lo
    begins = jnp.where(block_at == 0, 0.0, 1.0)
    ends = jnp.where(block_at == 2 * Z * n - 1, 0.0, 1.0)
    xe[0:16, :] = hprev[...].astype(F32) * begins
    xe[16 : 16 + count, :] = mel[...].astype(F32)
    xe[16 + count :, :] = hnext[...].astype(F32) * ends
    left = jnp.concatenate(
        [xe[15 : 15 + count, 128:256], xe[16 : 16 + count, :]], axis=1
    ).astype(BF16)
    right = jnp.concatenate([xe[0 : 16 + count, :], xe[1 : 17 + count, 0:128]], axis=1).astype(BF16)
    inside = jnp.where(
        lax.broadcasted_iota(jnp.int32, (16 + count, 1), 0) >= 16, jnp.ones((16 + count, 1), F32), begins
    )
    own_w1.wait()
    first_w.finish()
    for part in range(4):
        even[part] = gelu(jnp.dot(left, w1f[part], preferred_element_type=F32)).astype(BF16)
        odd[part] = gelu(jnp.dot(right, w1f[part], preferred_element_type=F32)) * inside
        if part == 0:
            conv_y.arrive(1)
            conv_y.arrive(2)
            conv.step(1)
            for k in (1, 2):
                qkv_y.arrive(k)
                qkv_z.arrive(k)
            conv_y.pass_on(0)
            qkv_y.pass_on(0)
        if part == 2:
            conv_y.arrive(3)
            conv_y.arrive(4)
            conv.step(2)
            for k in (3, 4):
                qkv_y.arrive(k)
                qkv_z.arrive(k)
            conv_y.pass_on(1)
            conv_y.pass_on(2)
    conv_y.arrive(5)
    conv_y.arrive(6)
    conv.step(3)
    for k in (5, 6):
        qkv_y.arrive(k)
        qkv_z.arrive(k)
    conv_y.pass_on(3)
    conv_y.pass_on(4)
    qkv_y.pass_on(1)
    qkv_y.pass_on(2)
    kvw.begin()
    conv_y.arrive(7)
    conv.step(Z // 2)
    qkv_y.arrive(7)
    qkv_z.arrive(7)
    for k in (5, 6, 7):
        conv_y.pass_on(k)
    qkv_y.pass_on(3)
    qkv_y.pass_on(4)
    proj_y.begin()
    proj_z.begin()
    conv.finish()
    conv_y.finish()

    rows2 = c2.shape[0] // 3
    wide = w1.shape[1]
    second = jnp.zeros((count, wide), F32)
    for part in range(4):
        taps = (
            odd[part, 15 : 15 + count, :].astype(BF16),
            even[part],
            odd[part, 16 : 16 + count, :].astype(BF16),
        )
        at = slice(2 * part, 2 * part + 2)
        blocks = (
            c2y[at, :, 0:rows2, :],
            jnp.concatenate([c2y[at, :, rows2:BY_Y, :], c2f[at, :, 0 : 2 * rows2 - BY_Y, :]], axis=2),
            c2f[at, :, 2 * rows2 - BY_Y :, :],
        )
        for tap in range(3):
            w = blocks[tap].reshape(4 * rows2, wide)
            second = second + jnp.dot(taps[tap], w, preferred_element_type=F32)
    hbox[me] = gelu(second).astype(BF16)
    share_h = Across(hbox.at[me], hbox, hb_s, hb_r)
    share_h.start()
    for k in (5, 6, 7):
        qkv_y.pass_on(k)
    kvw.arrive(1)
    kvw.arrive(2)
    share_h.relay()
    kvw.pass_on(0)
    own_g.wait()
    gains.finish()
    share_h.finish()
    parts = [hbox[k].astype(F32) for k in range(4)]
    center = sum(jnp.sum(p, axis=1, keepdims=True) for p in parts) / D
    parts = [p - center for p in parts]
    inv = lax.rsqrt(sum(jnp.sum(p * p, axis=1, keepdims=True) for p in parts) / D + 1e-05)
    for k in range(4):
        nbuf[k] = (parts[k] * inv * gf[k, 0:1, :]).astype(BF16)
    qkv_y.finish()
    qkv_z.finish()
    projected = jnp.zeros((count, qw.shape[1]), F32)
    for k in range(4):
        projected = projected + jnp.dot(
            nbuf[k], jnp.concatenate(
                [qwy[2 * k : 2 * k + 2], qwz[2 * k : 2 * k + 2]], axis=2
            ).reshape(4 * qw.shape[0], qw.shape[1]), preferred_element_type=F32
        )
    split = count // 2
    lower = lax.broadcasted_iota(jnp.int32, (split, 128), 1) < HD
    for i in range(n):
        pk[i, 0:count, :] = projected[:, i * 128 : (i + 1) * 128].astype(BF16)
        at = n * 128 + (i // 2) * 128
        a, b = projected[0:split, at : at + 128], projected[split:, at : at + 128]
        if i % 2 == 0:
            mixed_q = jnp.where(lower, a, pltpu.roll(b, HD, 1))
        else:
            mixed_q = jnp.where(lower, pltpu.roll(a, HD, 1), b)
        pk[i, count:, :] = mixed_q.astype(BF16)

    half = kv.shape[2] // n
    for i in range(n):
        own = jnp.logical_and(mirror, y == i)
        rows = pl.ds(pl.multiple_of(y * half, half), half)

        @pl.when(jnp.logical_not(own))
        def _():
            remote(pk.at[i, 0:half], kv.at[z, x_lo, rows], kv_s.at[i], kv_r.at[y], peers[i]).start()
            remote(pk.at[i, half:], qbox.at[y], q_s.at[i], q_r.at[y], peers[i]).start()

        @pl.when(own)
        def _():
            pltpu.make_async_copy(pk.at[i, 0:half], kv.at[z, c, rows], loc.at[0]).start()
            pltpu.make_async_copy(pk.at[i, half:], qbox.at[y], loc.at[1]).start()

    m[...] = jnp.full(m.shape, NEG, F32)
    l[...] = jnp.zeros(l.shape, F32)
    acc[...] = jnp.zeros(acc.shape, F32)

    for i in range(n):
        own = jnp.logical_and(mirror, y == i)
        rows = pl.ds(i * half, half)

        @pl.when(jnp.logical_not(own))
        def _():
            remote(pk.at[i, 0:half], kv.at[z, c, rows], kv_s.at[i], kv_r.at[i], peers[i]).wait()
            remote(pk.at[i, half:], qbox.at[i], q_s.at[i], q_r.at[i], peers[i]).wait()

        @pl.when(own)
        def _():
            pltpu.make_async_copy(pk.at[i, 0:half], kv.at[z, c, rows], loc.at[0]).wait()
            pltpu.make_async_copy(pk.at[i, half:], qbox.at[i], loc.at[1]).wait()

    width = kv.shape[2]

    def block(ref_z, core):
        return kv.at[ref_z, core]

    def send_up(t, zz):
        ref = block(zz, c) if t < Z // 2 - 1 else kv.at[zz, c, pl.ds(0, width // 2)]
        return remote(ref, ref, up_s.at[t], up_r.at[t], up)

    def send_down(t, zz):
        ref = block(zz, c) if t < Z // 2 - 1 else kv.at[zz, c, pl.ds(width // 2, width // 2)]
        return remote(ref, ref, dn_s.at[t], dn_r.at[t], down)

    def share(k, zz):
        return remote(block(zz, c), block(zz, c), co_s.at[k], co_r.at[k], twin)

    def taken(k, zz):
        return remote(block(zz, 1 - c), block(zz, 1 - c), co_s.at[k], co_r.at[k], twin)

    send_up(0, z).start()
    send_down(0, z).start()
    share(0, z).start()
    outw.start()

    lanes = lax.broadcasted_iota(jnp.int32, (half // 2, 128), 1)
    for i in range(n):
        raw = qbox[i].astype(F32) * 0.125
        qs[i * half : i * half + half // 2, :] = jnp.where(lanes < HD, raw, 0.0).astype(BF16)
        qs[i * half + half // 2 : (i + 1) * half, :] = jnp.where(
            lanes < HD, pltpu.roll(raw, HD, 1), 0.0
        ).astype(BF16)

    total = qs.shape[0]
    def process(zz, core):
        pairs = kv[zz, core]
        s = lax.dot_general(qs[...], pairs, (((1,), (1,)), ((), ())), preferred_element_type=F32)
        old = m[...]
        new = jnp.maximum(old, jnp.max(s, axis=1, keepdims=True))
        m[...] = new
        decay = jnp.exp(old - new)
        w = jnp.exp(s - jnp.concatenate([new] * (width // 128), axis=1))
        part = w[:, 0:128]
        for piece in range(1, width // 128):
            part = part + w[:, piece * 128 : (piece + 1) * 128]
        l[...] = l[...] * decay + part
        acc[...] = acc[...] * decay + jnp.dot(w.astype(BF16), pairs, preferred_element_type=F32)

    def both(zz, other, core):
        def turn(i, carry):
            process(jnp.where(i == 0, zz, other), core)
            return carry

        lax.fori_loop(0, 2, turn, 0)

    kvw.pass_on(1)
    kvw.pass_on(2)
    process(z, c)
    taken(0, z).wait_recv()
    process(z, 1 - c)
    far = Z // 2
    for t in range(1, far + 1):
        below = lax.rem(z + Z - t, Z)
        above = lax.rem(z + t, Z)
        send_up(t - 1, below).wait_recv()
        if t < far:
            send_up(t, below).start()
            share(2 * t - 1, below).start()
        send_down(t - 1, above).wait_recv()
        if t < far:
            send_down(t, above).start()
            share(2 * t, above).start()
        else:
            share(2 * t - 1, below).start()
        if t == 1:
            kvw.arrive(3)
            kvw.arrive(4)
        if t < far:
            both(below, above, c)
        else:
            process(below, c)
        if t == 1:
            for k in (1, 2):
                proj_y.arrive(k)
                proj_z.arrive(k)
        if t == 2:
            kvw.arrive(5)
            kvw.arrive(6)
            for k in (3, 4):
                proj_y.arrive(k)
                proj_z.arrive(k)
            proj_y.pass_on(0)
        if t == 3:
            for k in (5, 6):
                proj_y.arrive(k)
                proj_z.arrive(k)
            kvw.arrive(7)
            outw.relay()
        taken(2 * t - 1, below).wait_recv()
        if t < far:
            taken(2 * t, above).wait_recv()
            both(below, above, 1 - c)
        else:
            process(below, 1 - c)
        if t == 2:
            kvw.pass_on(3)
            kvw.pass_on(4)
            proj_y.pass_on(1)
            proj_y.pass_on(2)
        if t == 3:
            proj_y.arrive(7)
            proj_z.arrive(7)
            proj_y.pass_on(3)
            proj_y.pass_on(4)
            kvw.pass_on(5)

    quarter = half // 4
    low = lax.broadcasted_iota(jnp.int32, (quarter // 2, 128), 1) < HD
    head = (x_hi * 2 + x_lo) * n + y

    def give(j, q, slot, sem):
        k = 4 * j + q
        return remote(obuf.at[k], abox.at[slot], a_s.at[k], a_r.at[sem], device(j, q // 2, q % 2, z, c))

    for j in range(n):
        for q in range(4):
            k = 4 * j + q
            at = j * half + q * quarter
            top, bot = pl.ds(at, quarter // 2), pl.ds(at + quarter // 2, quarter // 2)
            first = pltpu.roll(acc[top, :] / jnp.sum(l[top, :], axis=1, keepdims=True), HD, 1)
            second = acc[bot, :] / jnp.sum(l[bot, :], axis=1, keepdims=True)
            obuf[k] = jnp.where(low, first, second).astype(BF16)
    for j in range(n):
        for q in range(4):
            own = jnp.logical_and(mirror, jnp.logical_and(y == j, me == q))

            @pl.when(jnp.logical_not(own))
            def _():
                give(j, q, head, head).start()

            @pl.when(own)
            def _():
                pltpu.make_async_copy(obuf.at[4 * j + q], abox.at[head], loc.at[0]).start()

    for k in (5, 6, 7):
        proj_y.pass_on(k)
    kvw.pass_on(6)

    for t in range(far):
        send_up(t, z).wait_send()
        send_down(t, z).wait_send()
    for k in range(2 * far):
        share(k, z).wait_send()
    outw.finish()
    own_w.wait()

    for h in range(4 * n):
        own = jnp.logical_and(mirror, head == h)

        @pl.when(jnp.logical_not(own))
        def _():
            remote(obuf.at[h], abox.at[h], a_s.at[h], a_r.at[h], twin).wait_recv()

        @pl.when(own)
        def _():
            pltpu.make_async_copy(obuf.at[h], abox.at[h], loc.at[0]).wait()

    for pair in range(2 * n):
        a = abox[2 * pair].astype(F32)
        b = abox[2 * pair + 1].astype(F32)
        cols = slice(pair * 128, (pair + 1) * 128)
        att[0 : quarter // 2, cols] = jnp.where(low, a, pltpu.roll(b, HD, 1)).astype(BF16)
        att[quarter // 2 :, cols] = jnp.where(low, pltpu.roll(a, HD, 1), b).astype(BF16)

    mixed = jnp.dot(
        att[...], owf[...].reshape(4 * ow.shape[0], ow.shape[1]), preferred_element_type=F32
    )
    tokens = quarter // 2
    pieces = []
    mine = pl.ds(pl.multiple_of(me * quarter, quarter), quarter)
    own_rows = jnp.concatenate([hbox[k, mine, :].astype(F32) for k in range(4)], axis=1)
    gain = jnp.concatenate([gf[k, 1:2, :] for k in range(4)], axis=1)
    for k in range(D // 128):
        at = slice(k * 128, (k + 1) * 128)
        res[k] = own_rows[:, at] + mixed[:, at]
        pieces.append(
            (res.at[k][pl.ds(0, tokens, stride=2), :] + res.at[k][pl.ds(1, tokens, stride=2), :]) * 0.5
        )
    pooled = jnp.concatenate(pieces, axis=1)
    pbox[me] = normal(pooled, gain).astype(BF16)
    gather = Across(pbox.at[me], pbox, pb_s, pb_r)
    gather.start()
    gather.relay()
    kvw.pass_on(7)
    proj_y.finish()
    proj_z.finish()
    gather.finish()

    post = pbox[...].reshape(4 * tokens, pbox.shape[2])
    embedded = jnp.dot(
        post,
        jnp.concatenate([pwy[...], pwz[...]], axis=2).reshape(2 * Z * pw.shape[0], pw.shape[1]),
        preferred_element_type=F32,
    ).astype(BF16)
    widened = embedded.astype(F32)
    sbox[me] = jnp.broadcast_to(
        jnp.sum(widened * widened, axis=1, keepdims=True), (4 * tokens, 128)
    )
    squares = Across(sbox.at[me], sbox, sb_s, sb_r)
    squares.start()
    ebox[x_lo] = (widened * rg[0:1, :]).astype(BF16)
    side = device(y, x_hi, c, z, 1 - x_lo)

    def lend(b):
        return remote(ebox.at[b], ebox.at[b], e_s.at[0], e_r.at[0], side)

    def hand(src):
        return remote(src, precv, e_s.at[1], e_r.at[1], side)

    def swap(k):
        return remote(tsend.at[k], trecv.at[k], t_s.at[k], t_r.at[k], twin)

    def over(k):
        return remote(csend.at[k], crecv.at[k], c_s.at[k], c_r.at[k], far_dev)

    lend(x_lo).start()
    kvw.finish()
    cols = pw.shape[1]
    part_c = cols // 2

    def columns(rows, a, b):
        at = pl.ds(pl.multiple_of((a * 2 + b) * part_c, part_c), part_c)
        return jnp.dot(ebox[rows], kwf[:, :, :, at].reshape(cols, part_c), preferred_element_type=F32)

    for k in range(2):
        rows = x_lo if k == 0 else 1 - x_lo
        if k == 1:
            lend(rows).wait_recv()
        tsend[k, 0] = columns(rows, 1 - x_hi, 1 - c).astype(BF16)
        tsend[k, 1] = columns(rows, x_hi, 1 - c).astype(BF16)
        swap(k).start()
        keep[k, 0] = columns(rows, 1 - x_hi, c)
        keep[k, 1] = columns(rows, x_hi, c)
        if k == 0:
            squares.relay()
        swap(k).wait_recv()
        csend[k] = (keep[k, 0] + trecv[k, 0].astype(F32)).astype(BF16)
        over(k).start()
        keep[k, 1] = keep[k, 1] + trecv[k, 1].astype(F32)
    squares.finish()
    scale = lax.rsqrt((sbox[0] + sbox[1] + sbox[2] + sbox[3]) / DL + 1e-06)

    def turned(value, h, base):
        value = value * scale
        at = pl.ds(pl.multiple_of(base + h * LHD, LHD), LHD)
        out[:, at] = (value * cs[...] + pltpu.roll(value, HD, 1) * sn[...]).astype(BF16)

    heads_half = part_c // LHD
    over(0).wait_recv()
    for h in range(heads_half):
        at = slice(h * LHD, (h + 1) * LHD)
        turned(keep[0, 1, :, at] + crecv[0, :, at].astype(F32), h, x_lo * part_c)
    over(1).wait_recv()
    psend[...] = (keep[1, 1] + crecv[1].astype(F32)).astype(BF16)
    hand(psend).start()
    hand(psend).wait_recv()
    for h in range(heads_half):
        at = slice(h * LHD, (h + 1) * LHD)
        turned(precv[:, at].astype(F32), h, (1 - x_lo) * part_c)

    lend(x_lo).wait_send()
    hand(psend).wait_send()
    over(1).wait_send()
    edge_next.wait_send()
    edge_prev.wait_send()
    swap(0).wait_send()
    swap(1).wait_send()
    over(0).wait_send()
    for j in range(n):
        for q in range(4):
            own = jnp.logical_and(mirror, jnp.logical_and(y == j, me == q))

            @pl.when(jnp.logical_not(own))
            def _():
                give(j, q, head, head).wait_send()


def layer(mel, w1, c2, gn, qw, ow, pw, kw, rg, cs, sn):
    frames = mel.shape[0]
    n = lax.axis_size("tm")
    Z = lax.axis_size("section") // 2
    total = frames * n
    tokens = frames // 2
    quarter = frames // 4
    cols = pw.shape[1]
    wide = w1.shape[1]
    sem = pltpu.SemaphoreType.DMA
    vm = pl.BlockSpec(memory_space=pltpu.VMEM)
    V = pltpu.VMEM
    half = Z // 2
    ring = [sem((half,))] * 8 + [sem((Z,))] * 2
    return pl.pallas_call(
        layer_kernel,
        out_shape=jax.ShapeDtypeStruct((tokens, cols), BF16),
        in_specs=[vm] * 7 + [pl.BlockSpec(memory_space=pl.ANY)] + [vm] * 3,
        out_specs=vm,
        scratch_shapes=[
            V((16, mel.shape[1]), BF16),
            V((16, mel.shape[1]), BF16),
            V((4,) + w1.shape, BF16),
            V((4,) + gn.shape, F32),
            V((Z, 2, c2.shape[0] - BY_Y, wide), BF16),
            V((Z, 2, BY_Y, wide), BF16),
            V((Z, 2, ROWS_Y, qw.shape[1]), BF16),
            V((Z, 2, qw.shape[0] - ROWS_Y, qw.shape[1]), BF16),
            V((2, kw.shape[0], kw.shape[1] // 2), BF16),
            V((frames + 32, mel.shape[1]), F32),
            V((4, frames, wide), BF16),
            V((4, frames + 16, wide), F32),
            V((4, frames, wide), BF16),
            V((4, frames, wide), BF16),
            V((n, frames + tokens, 128), BF16),
            V((Z, 2, total, 128), BF16),
            V((n, tokens, 128), BF16),
            V((total, 128), BF16),
            V((total, 128), F32),
            V((total, 128), F32),
            V((total, 128), F32),
            V((16, quarter // 2, 128), BF16),
            V((16, quarter // 2, 128), BF16),
            V((quarter, ow.shape[0] * 4), BF16),
            V((ow.shape[1] // 128, quarter, 128), F32),
            V((4,) + ow.shape, BF16),
            V((Z, 2, ROWS_Y, cols), BF16),
            V((Z, 2, pw.shape[0] - ROWS_Y, cols), BF16),
            V((Z, 2, kw.shape[0], kw.shape[1] // 2), BF16),
            V((4, quarter // 2, ow.shape[1]), BF16),
            V((4, tokens, 128), F32),
            V((2, tokens, cols), BF16),
            V((2, 2, tokens, cols // 2), F32),
            V((2, 2, tokens, cols // 2), BF16),
            V((2, 2, tokens, cols // 2), BF16),
            V((2, tokens, cols // 2), BF16),
            V((2, tokens, cols // 2), BF16),
            V((tokens, cols // 2), BF16),
            V((tokens, cols // 2), BF16),
            sem((n,)), sem((n,)), sem((n,)), sem((n,)), sem((20,)),
            sem((half,)), sem((half,)), sem((half,)), sem((half,)), sem((Z,)), sem((Z,)), sem((16,)), sem((16,)),
            sem((3,)), sem((3,)), sem((3,)), sem((3,)), sem((3,)), sem((3,)), sem((2,)), sem((2,)), sem((2,)), sem((2,)), sem((2,)), sem((2,)),
            sem((2,)), sem((2,)), sem((3,)), sem((3,)), sem((3,)), sem((3,)), sem((3,)), sem((3,)),
        ]
        + ring
        + ([sem((half,))] * 4 + [sem((1,))] * 2 + [sem((Z,))] * 8) * 4
        + ([sem((half,))] * 4 + [sem((1,))] * 2) * 2,
        compiler_params=pltpu.CompilerParams(
            collective_id=1, has_side_effects=True, vmem_limit_bytes=60 * 2**20
        ),
    )(mel, w1, c2, gn, qw, ow, pw, kw, rg, cs, sn)


def tables(rows, cols):
    row_start = (lax.axis_index("tm") * lax.axis_size("section") + lax.axis_index("section")) * rows
    positions = (row_start + jnp.arange(rows, dtype=jnp.int32)).astype(F32)
    within = jnp.arange(LHD, dtype=jnp.int32)
    freq = jnp.power(10000.0, -2.0 * (within % (LHD // 2)).astype(F32) / LHD)
    angle = positions[:, None] * freq[None, :]
    keys = lax.axis_index("mp") * cols < KVH * LHD
    sines = jnp.where(within < LHD // 2, -1.0, 1.0) * jnp.sin(angle)
    return jnp.where(keys, jnp.cos(angle), 1.0), jnp.where(keys, sines, 0.0)


def shards(
    mel_frames,
    conv1_weight,
    conv2_weight,
    attn_gain,
    qkv_weight,
    out_weight,
    post_gain,
    proj_weight,
    rms_gain,
    kv_weight,
):
    frames = mel_frames.shape[0] // 2
    bins, wide = conv1_weight.shape[1:]
    rows, _, width = qkv_weight.shape
    heads = width // HD
    split = qkv_weight.reshape(rows, 3, heads, HD)
    pairs = jnp.stack([split[:, 1], split[:, 2]], axis=2).reshape(rows, 2 * width)
    weight = jnp.concatenate([pairs, qkv_weight[:, 0]], axis=1)
    gains = jnp.pad(jnp.stack([attn_gain, post_gain]), ((0, 6), (0, 0)))
    cs, sn = tables(frames // 2, proj_weight.shape[1])
    return layer(
        mel_frames.reshape(frames, 2 * bins),
        conv1_weight.reshape(3 * bins, wide),
        conv2_weight.reshape(-1, wide),
        gains,
        weight,
        out_weight,
        proj_weight,
        kv_weight,
        rms_gain.reshape(1, -1),
        cs,
        sn,
    )


def solution(mesh):
    return jax.shard_map(
        shards,
        mesh=mesh,
        in_specs=(
            P(("tm", "section"), None),
            P(None, None, "mp"),
            P(None, "section", "mp"),
            P("mp"),
            P("section", None, "mp"),
            P("mp", None),
            P("mp"),
            P("section", "mp"),
            P("mp"),
            P(("mp", "section"), None),
        ),
        out_specs=P(("tm", "section"), "mp"),
        check_vma=False,
    )
```

```python
import functools
import math

import jax
import jax.numpy as jnp
from jax import lax
from jax.experimental import pallas as pl
from jax.experimental.pallas import tpu as pltpu
from jax.sharding import PartitionSpec as P

D = 1280
HD = 64
DL = 4096
KVH = 16
LHD = 128
MESH = pl.DeviceIdType.MESH
F32 = jnp.float32
BF16 = jnp.bfloat16


def place():
    mp, sec = lax.axis_index("mp"), lax.axis_index("section")
    return lax.axis_index("tm"), mp // 2, mp % 2, sec // 2, sec % 2


def device(y, x_hi, c, z, x_lo):
    return {"tm": y, "mp": x_hi * 2 + c, "section": z * 2 + x_lo}


def remote(src, dst, send, recv, target):
    return pltpu.make_async_remote_copy(
        src_ref=src, dst_ref=dst, send_sem=send, recv_sem=recv, device_id=target, device_id_type=MESH
    )


NEG = -1e30
BY_Y = 128
ROWS_Y = 64


def line(step, Z, Y):
    y, x_hi, c, z, x_lo = place()
    sections = 2 * Z
    at = lax.rem(y * sections + z * 2 + x_lo + step + Y * sections, Y * sections)
    return {"tm": at // sections, "mp": x_hi * 2 + c, "section": lax.rem(at, sections)}


def gelu(x):
    return 0.5 * x * (1.0 + lax.erf(x * math.sqrt(0.5)))


def greet(Z, Y):
    y, x_hi, c, z, x_lo = place()
    barrier = pltpu.get_barrier_semaphore()
    for step in (1, Z - 1):
        pl.semaphore_signal(
            barrier, inc=1, device_id=device(y, x_hi, c, lax.rem(z + step, Z), x_lo), device_id_type=MESH
        )
    for dy in range(Y):
        for k in range(8):
            if dy == 0 and k == 0:
                continue
            a, b, d = k // 4, (k // 2) % 2, k % 2
            other = device(
                lax.rem(y + dy, Y), lax.rem(x_hi + a, 2), lax.rem(c + b, 2), z, lax.rem(x_lo + d, 2)
            )
            pl.semaphore_signal(barrier, inc=1, device_id=other, device_id_type=MESH)
    pl.semaphore_signal(barrier, inc=1, device_id=line(jnp.where(x_lo == 1, 1, -1), Z, Y), device_id_type=MESH)
    pl.semaphore_wait(barrier, 8 * Y + 2)


class Across:
    def __init__(self, src, buf, send, recv, near=False):
        y, x_hi, c, z, x_lo = place()
        self.buf, self.send, self.recv, self.src = buf, send, recv, src
        self.me, self.twin, self.far, self.both = (
            x_hi * 2 + c, x_hi * 2 + 1 - c, (1 - x_hi) * 2 + c, (1 - x_hi) * 2 + 1 - c
        )
        self.to_twin = device(y, x_hi, 1 - c, z, x_lo)
        self.to_far = device(y, 1 - x_hi, c, z, 1 - x_lo if near else x_lo)

    def copy(self, k, src, slot, target):
        return remote(src, self.buf.at[slot], self.send.at[k], self.recv.at[k], target)

    def start(self):
        self.copy(1, self.src, self.me, self.to_far).start()
        self.copy(0, self.src, self.me, self.to_twin).start()

    def relay(self):
        self.copy(1, self.buf.at[self.far], self.far, self.to_far).wait_recv()
        self.copy(2, self.buf.at[self.far], self.far, self.to_twin).start()

    def finish(self):
        self.copy(0, self.buf.at[self.twin], self.twin, self.to_twin).wait_recv()
        self.copy(2, self.buf.at[self.both], self.both, self.to_twin).wait_recv()
        for k in range(3):
            self.copy(k, self.buf.at[self.me], self.me, self.to_twin).wait_send()


class Sections:
    def __init__(self, src, buf, us, ur, ds, dr, ous, our, ods, odr, xs, xr, loc, h0):
        y, x_hi, c, z, x_lo = place()
        self.Z = buf.shape[0]
        self.src, self.buf, self.z, self.x = src, buf, z, x_lo
        self.s = (us, ur, ds, dr, ous, our, ods, odr, xs, xr)
        self.loc = loc
        self.h0 = h0
        self.hi = pl.ds(h0, src.shape[0] - h0)
        self.up = device(y, x_hi, c, lax.rem(z + 1, self.Z), x_lo)
        self.down = device(y, x_hi, c, lax.rem(z + self.Z - 1, self.Z), x_lo)
        self.side = device(y, x_hi, c, z, 1 - x_lo)

    def below(self, t):
        return lax.rem(self.z + self.Z - t, self.Z)

    def above(self, t):
        return lax.rem(self.z + t, self.Z)

    def ring(self, kind, t, zz, src=None):
        us, ur, ds, dr, ous, our, ods, odr, xs, xr = self.s
        own = kind in "ud"
        count = self.src.shape[0] if own else self.h0
        cut = (count // 2 + 15) // 16 * 16
        if t < self.Z // 2 - 1:
            rows = pl.ds(0, count)
        else:
            rows = pl.ds(0, cut) if kind[-1] == "u" else pl.ds(cut, count - cut)
        ref = self.buf.at[zz, self.x if own else 1 - self.x, rows]
        send, recv, to = {
            "u": (us, ur, self.up), "d": (ds, dr, self.down), "ou": (ous, our, self.up), "od": (ods, odr, self.down)
        }[kind]
        return remote(ref if src is None else src, ref, send.at[t], recv.at[t], to)

    def whole(self, x):
        us, ur, ds, dr, ous, our, ods, odr, xs, xr = self.s
        return remote(self.src, self.buf.at[self.z, x], xs.at[0], xr.at[0], self.side)

    def forward(self, k, zz, x):
        us, ur, ds, dr, ous, our, ods, odr, xs, xr = self.s
        ref = self.buf.at[zz, x, self.hi]
        return remote(ref, ref, xs.at[k], xr.at[k], self.side)

    def local(self):
        return pltpu.make_async_copy(self.src, self.buf.at[self.z, self.x], self.loc)

    def start(self):
        self.local().start()
        self.whole(self.x).start()
        self.ring("u", 0, self.z, self.src).start()
        self.ring("d", 0, self.z, self.src).start()

    def start_other(self):
        self.whole(1 - self.x).wait_recv()
        self.ring("ou", 0, self.z).start()
        self.ring("od", 0, self.z).start()

    def step(self, t):
        far = self.Z // 2
        for kind, zz, k in (("u", self.below(t), 2 * t - 1), ("d", self.above(t), 2 * t)):
            self.ring(kind, t - 1, zz).wait_recv()
            if t < far:
                self.ring(kind, t, zz).start()
                self.forward(k, zz, self.x).start()
        if t == far:
            self.forward(2 * t - 1, self.below(t), self.x).start()
        for kind, zz in (("ou", self.below(t)), ("od", self.above(t))):
            self.ring(kind, t - 1, zz).wait_recv()
            if t < far:
                self.ring(kind, t, zz).start()

    def finish(self):
        far = self.Z // 2
        for t in range(1, far + 1):
            self.forward(2 * t - 1, self.below(t), 1 - self.x).wait_recv()
            if t < far:
                self.forward(2 * t, self.above(t), 1 - self.x).wait_recv()
        self.local().wait()
        self.whole(self.x).wait_send()
        for t in range(far):
            for kind in ("u", "d", "ou", "od"):
                self.ring(kind, t, self.z).wait_send()
        for k in range(1, 2 * far):
            self.forward(k, self.z, self.x).wait_send()


class Quarters:
    def __init__(self, src, buf, us, ur, ds, dr, xs, xr, yus, yur, yds, ydr, rus, rur, rds, rdr, loc, other=None, Y=4):
        y, x_hi, c, z, x_lo = place()
        self.Z, self.Y = buf.shape[0], Y
        self.rows = buf.shape[2] // Y
        self.other = src if other is None else other
        self.src, self.buf, self.z, self.x, self.y = src, buf, z, x_lo, y if Y > 1 else 0
        self.s = (us, ur, ds, dr, xs, xr, yus, yur, yds, ydr, rus, rur, rds, rdr)
        self.loc = loc
        self.up = device(y, x_hi, c, lax.rem(z + 1, self.Z), x_lo)
        self.down = device(y, x_hi, c, lax.rem(z + self.Z - 1, self.Z), x_lo)
        self.side = device(y, x_hi, c, z, 1 - x_lo)
        self.yn, self.yp, self.yf = lax.rem(y + 1, 4), lax.rem(y + 3, 4), lax.rem(y + 2, 4)
        self.next = device(self.yn, x_hi, c, z, x_lo)
        self.prev = device(self.yp, x_hi, c, z, x_lo)

    def part(self, q):
        if self.Y == 1:
            return pl.ds(0, self.rows)
        return pl.ds(pl.multiple_of(q * self.rows, self.rows), self.rows)

    def zs(self, k):
        if k % 2:
            return lax.rem(self.z + self.Z - (k + 1) // 2, self.Z)
        return lax.rem(self.z + k // 2, self.Z)

    def ring(self, kind, t, zz):
        us, ur, ds, dr = self.s[:4]
        shard = slice(None) if t < self.Z // 2 - 1 else (0 if kind == "u" else 1)
        ref = self.buf.at[zz, shard, self.part(self.y)]
        if kind == "u":
            return remote(ref, ref, us.at[t], ur.at[t], self.up)
        return remote(ref, ref, ds.at[t], dr.at[t], self.down)

    def cross(self, x):
        xs, xr = self.s[4:6]
        at = self.part(self.y)
        return remote(self.other.at[at], self.buf.at[self.z, x, at], xs.at[0], xr.at[0], self.side)

    def local(self):
        return pltpu.make_async_copy(self.src, self.buf.at[self.z, self.x], self.loc)

    def spread(self, kind, k, quarter):
        yus, yur, yds, ydr = self.s[6:10]
        if k == 0:
            ref = self.buf.at[self.z, 1 - self.x, self.part(quarter)]
        else:
            ref = self.buf.at[self.zs(k), :, self.part(quarter)]
        if kind == "n":
            return remote(ref, ref, yus.at[k], yur.at[k], self.next)
        return remote(ref, ref, yds.at[k], ydr.at[k], self.prev)

    def relay(self, kind, k, quarter):
        rus, rur, rds, rdr = self.s[10:14]
        if kind == "n":
            ref = self.buf.at[self.zs(k), (1 - self.x) if k == 0 else 0, self.part(quarter)]
            return remote(ref, ref, rus.at[k], rur.at[k], self.next)
        ref = self.buf.at[self.zs(k), 1, self.part(quarter)]
        return remote(ref, ref, rds.at[k], rdr.at[k], self.prev)

    def start(self):
        self.cross(self.x).start()
        self.local().start()

    def begin(self):
        self.local().wait()
        self.cross(1 - self.x).wait_recv()
        self.ring("u", 0, self.z).start()
        self.ring("d", 0, self.z).start()
        if self.Y > 1:
            self.spread("n", 0, self.y).start()
            self.spread("p", 0, self.y).start()

    def fetch(self, k):
        last = (k + 1) // 2 == self.Z // 2
        for kind in "ud" if last else ("u" if k % 2 else "d"):
            self.ring(kind, (k + 1) // 2 - 1, self.zs(k)).wait_recv()
        if self.Y > 1:
            self.spread("n", k, self.y).start()
            self.spread("p", k, self.y).start()

    def onward(self, k):
        t = (k + 1) // 2
        if t < self.Z // 2:
            self.ring("u" if k % 2 else "d", t, self.zs(k)).start()

    def arrive(self, k):
        self.fetch(k)
        self.onward(k)

    def pass_on(self, k):
        self.spread("n", k, self.yp).wait_recv()
        self.relay("n", k, self.yp).start()
        self.spread("p", k, self.yn).wait_recv()
        if k:
            self.relay("p", k, self.yn).start()

    def finish(self):
        far = self.Z // 2
        turns = range(2 * far if self.Y > 1 else 0)
        for k in turns:
            self.relay("n", k, self.yf).wait_recv()
            if k:
                self.relay("p", k, self.yf).wait_recv()
        self.cross(self.x).wait_send()
        for t in range(far):
            self.ring("u", t, self.z).wait_send()
            self.ring("d", t, self.z).wait_send()
        for k in turns:
            self.spread("n", k, self.y).wait_send()
            self.spread("p", k, self.y).wait_send()
            self.relay("n", k, self.y).wait_send()
            if k:
                self.relay("p", k, self.y).wait_send()


def normal(rows, gain):
    center = jnp.mean(rows, axis=-1, keepdims=True)
    spread = jnp.mean(jnp.square(rows - center), axis=-1, keepdims=True)
    return (rows - center) * lax.rsqrt(spread + 1e-05) * gain


def layer_kernel(
    mel, w1, c2, gn, qw, ow, pw, kw, rg, cs, sn, out,
    hprev, hnext, w1f, gf, c2f, c2y, qwy, qwz, kwa, xe, even, odd, hbox, nbuf, pk,
    kv, qbox, qs, m, l, acc, obuf, abox, att, res, owf, pwy, pwz, kwf, pbox, sbox, ebox, keep, tsend, trecv, csend, crecv, psend, precv,
    kv_s, kv_r, q_s, q_r, loc, up_s, up_r, dn_s, dn_r, co_s, co_r, a_s, a_r,
    ow_s, ow_r, pb_s, pb_r, sb_s, sb_r, t_s, t_r, c_s, c_r, e_s, e_r, pc_s, pc_r,
    h_s, h_r, w1_s, w1_r, g_s, g_r, hb_s, hb_r,
    *rings,
):
    y, x_hi, c, z, x_lo = place()
    Z = kv.shape[0]
    n = qbox.shape[0]
    me = x_hi * 2 + c
    up = device(y, x_hi, c, lax.rem(z + 1, Z), x_lo)
    down = device(y, x_hi, c, lax.rem(z + Z - 1, Z), x_lo)
    twin = device(y, x_hi, 1 - c, z, x_lo)
    far_dev = device(y, 1 - x_hi, c, z, x_lo)
    peers = [device(i, x_hi, x_lo, z, c) for i in range(n)]
    mirror = c == x_lo

    outw = Across(ow, owf, ow_s, ow_r, True)
    quarters, pairs = rings[10:66], rings[66:78]
    none = (None,) * 8
    proj_y = Quarters(pw.at[pl.ds(0, ROWS_Y)], pwy, *quarters[0:14], loc.at[3])
    proj_z = Quarters(pw.at[pl.ds(ROWS_Y, pw.shape[0] - ROWS_Y)], pwz, *pairs[0:6], *none, loc.at[10], Y=1)
    qkv_y = Quarters(qw.at[pl.ds(0, ROWS_Y)], qwy, *quarters[14:28], loc.at[7])
    qkv_z = Quarters(qw.at[pl.ds(ROWS_Y, qw.shape[0] - ROWS_Y)], qwz, *pairs[6:12], *none, loc.at[11], Y=1)
    conv = Sections(c2.at[pl.ds(BY_Y, c2.shape[0] - BY_Y)], c2f, *rings[0:10], loc.at[6], 48)
    conv_y = Quarters(c2.at[pl.ds(0, BY_Y)], c2y, *quarters[28:42], loc.at[2])
    kvw = Quarters(kwa.at[x_lo], kwf, *quarters[42:56], loc.at[4], kwa.at[1 - x_lo])
    first_w = Across(w1, w1f, w1_s, w1_r, True)
    gains = Across(gn, gf, g_s, g_r, True)
    own_w1 = pltpu.make_async_copy(w1, w1f.at[me], loc.at[8])
    own_g = pltpu.make_async_copy(gn, gf.at[me], loc.at[9])
    own_w1.start()
    own_g.start()
    wide_c = kw.shape[1] // 8
    arrange = [
        pltpu.make_async_copy(
            kw.at[:, pl.ds((2 * k + h) * wide_c, wide_c)], kwa.at[h, :, pl.ds(k * wide_c, wide_c)], loc.at[12 + 4 * h + k]
        )
        for h in range(2)
        for k in range(4)
    ]
    for copy in arrange:
        copy.start()
    count = mel.shape[0]
    greet(Z, n)

    tail16, head16 = pl.ds(count - 16, 16), pl.ds(0, 16)
    edge_next = remote(mel.at[tail16], hprev, h_s.at[0], h_r.at[0], line(1, Z, n))
    edge_prev = remote(mel.at[head16], hnext, h_s.at[1], h_r.at[1], line(-1, Z, n))
    conv_y.start()
    conv.start()
    first_w.start()
    edge_next.start()
    edge_prev.start()
    gains.start()
    qkv_y.start()
    qkv_z.start()
    conv_y.begin()
    conv.start_other()
    qkv_y.begin()
    qkv_z.begin()
    first_w.relay()
    gains.relay()
    for copy in arrange:
        copy.wait()
    kvw.start()
    proj_y.start()
    proj_z.start()
    own_w = pltpu.make_async_copy(ow, owf.at[me], loc.at[5])
    own_w.start()
    edge_next.wait_recv()
    edge_prev.wait_recv()
    block_at = y * 2 * Z + z * 2 + x_lo
    begins = jnp.where(block_at == 0, 0.0, 1.0)
    ends = jnp.where(block_at == 2 * Z * n - 1, 0.0, 1.0)
    xe[0:16, :] = hprev[...].astype(F32) * begins
    xe[16 : 16 + count, :] = mel[...].astype(F32)
    xe[16 + count :, :] = hnext[...].astype(F32) * ends
    left = jnp.concatenate(
        [xe[15 : 15 + count, 128:256], xe[16 : 16 + count, :]], axis=1
    ).astype(BF16)
    right = jnp.concatenate([xe[0 : 16 + count, :], xe[1 : 17 + count, 0:128]], axis=1).astype(BF16)
    inside = jnp.where(
        lax.broadcasted_iota(jnp.int32, (16 + count, 1), 0) >= 16, jnp.ones((16 + count, 1), F32), begins
    )
    own_w1.wait()
    first_w.finish()
    for part in range(4):
        even[part] = gelu(jnp.dot(left, w1f[part], preferred_element_type=F32)).astype(BF16)
        odd[part] = gelu(jnp.dot(right, w1f[part], preferred_element_type=F32)) * inside
        if part == 0:
            conv_y.arrive(1)
            conv_y.arrive(2)
            conv.step(1)
            for k in (1, 2):
                qkv_y.arrive(k)
                qkv_z.arrive(k)
            conv_y.pass_on(0)
            qkv_y.pass_on(0)
        if part == 2:
            conv_y.arrive(3)
            conv_y.arrive(4)
            conv.step(2)
            for k in (3, 4):
                qkv_y.arrive(k)
                qkv_z.arrive(k)
            conv_y.pass_on(1)
            conv_y.pass_on(2)
    conv_y.arrive(5)
    conv_y.arrive(6)
    conv.step(3)
    for k in (5, 6):
        qkv_y.arrive(k)
        qkv_z.arrive(k)
    conv_y.pass_on(3)
    conv_y.pass_on(4)
    qkv_y.pass_on(1)
    qkv_y.pass_on(2)
    conv_y.arrive(7)
    conv.step(Z // 2)
    qkv_y.arrive(7)
    qkv_z.arrive(7)
    for k in (5, 6, 7):
        conv_y.pass_on(k)
    kvw.begin()
    qkv_y.pass_on(3)
    qkv_y.pass_on(4)
    conv.finish()
    conv_y.finish()
    proj_y.begin()
    proj_z.begin()

    rows2 = c2.shape[0] // 3
    wide = w1.shape[1]
    second = jnp.zeros((count, wide), F32)
    for part in range(4):
        taps = (
            odd[part, 15 : 15 + count, :].astype(BF16),
            even[part],
            odd[part, 16 : 16 + count, :].astype(BF16),
        )
        at = slice(2 * part, 2 * part + 2)
        blocks = (
            c2y[at, :, 0:rows2, :],
            jnp.concatenate([c2y[at, :, rows2:BY_Y, :], c2f[at, :, 0 : 2 * rows2 - BY_Y, :]], axis=2),
            c2f[at, :, 2 * rows2 - BY_Y :, :],
        )
        for tap in range(3):
            w = blocks[tap].reshape(4 * rows2, wide)
            second = second + jnp.dot(taps[tap], w, preferred_element_type=F32)
    hbox[me] = gelu(second).astype(BF16)
    share_h = Across(hbox.at[me], hbox, hb_s, hb_r)
    share_h.start()
    for k in (5, 6, 7):
        qkv_y.pass_on(k)
    kvw.arrive(1)
    kvw.arrive(2)
    share_h.relay()
    kvw.pass_on(0)
    own_g.wait()
    gains.finish()
    share_h.finish()
    parts = [hbox[k].astype(F32) for k in range(4)]
    center = sum(jnp.sum(p, axis=1, keepdims=True) for p in parts) / D
    parts = [p - center for p in parts]
    inv = lax.rsqrt(sum(jnp.sum(p * p, axis=1, keepdims=True) for p in parts) / D + 1e-05)
    for k in range(4):
        nbuf[k] = (parts[k] * inv * gf[k, 0:1, :]).astype(BF16)
    qkv_y.finish()
    qkv_z.finish()
    projected = jnp.zeros((count, qw.shape[1]), F32)
    for k in range(4):
        projected = projected + jnp.dot(
            nbuf[k], jnp.concatenate(
                [qwy[2 * k : 2 * k + 2], qwz[2 * k : 2 * k + 2]], axis=2
            ).reshape(4 * qw.shape[0], qw.shape[1]), preferred_element_type=F32
        )
    split = count // 2
    lower = lax.broadcasted_iota(jnp.int32, (split, 128), 1) < HD
    for i in range(n):
        pk[i, 0:count, :] = projected[:, i * 128 : (i + 1) * 128].astype(BF16)
        at = n * 128 + (i // 2) * 128
        a, b = projected[0:split, at : at + 128], projected[split:, at : at + 128]
        if i % 2 == 0:
            mixed_q = jnp.where(lower, a, pltpu.roll(b, HD, 1))
        else:
            mixed_q = jnp.where(lower, pltpu.roll(a, HD, 1), b)
        pk[i, count:, :] = mixed_q.astype(BF16)

    half = kv.shape[2] // n
    for i in range(n):
        own = jnp.logical_and(mirror, y == i)
        rows = pl.ds(pl.multiple_of(y * half, half), half)

        @pl.when(jnp.logical_not(own))
        def _():
            remote(pk.at[i, 0:half], kv.at[z, x_lo, rows], kv_s.at[i], kv_r.at[y], peers[i]).start()
            remote(pk.at[i, half:], qbox.at[y], q_s.at[i], q_r.at[y], peers[i]).start()

        @pl.when(own)
        def _():
            pltpu.make_async_copy(pk.at[i, 0:half], kv.at[z, c, rows], loc.at[0]).start()
            pltpu.make_async_copy(pk.at[i, half:], qbox.at[y], loc.at[1]).start()

    m[...] = jnp.full(m.shape, NEG, F32)
    l[...] = jnp.zeros(l.shape, F32)
    acc[...] = jnp.zeros(acc.shape, F32)

    for i in range(n):
        own = jnp.logical_and(mirror, y == i)
        rows = pl.ds(i * half, half)

        @pl.when(jnp.logical_not(own))
        def _():
            remote(pk.at[i, 0:half], kv.at[z, c, rows], kv_s.at[i], kv_r.at[i], peers[i]).wait()
            remote(pk.at[i, half:], qbox.at[i], q_s.at[i], q_r.at[i], peers[i]).wait()

        @pl.when(own)
        def _():
            pltpu.make_async_copy(pk.at[i, 0:half], kv.at[z, c, rows], loc.at[0]).wait()
            pltpu.make_async_copy(pk.at[i, half:], qbox.at[i], loc.at[1]).wait()

    width = kv.shape[2]

    def block(ref_z, core):
        return kv.at[ref_z, core]

    def send_up(t, zz):
        ref = block(zz, c) if t < Z // 2 - 1 else kv.at[zz, c, pl.ds(0, width // 2)]
        return remote(ref, ref, up_s.at[t], up_r.at[t], up)

    def send_down(t, zz):
        ref = block(zz, c) if t < Z // 2 - 1 else kv.at[zz, c, pl.ds(width // 2, width // 2)]
        return remote(ref, ref, dn_s.at[t], dn_r.at[t], down)

    def share(k, zz):
        return remote(block(zz, c), block(zz, c), co_s.at[k], co_r.at[k], twin)

    def taken(k, zz):
        return remote(block(zz, 1 - c), block(zz, 1 - c), co_s.at[k], co_r.at[k], twin)

    send_up(0, z).start()
    send_down(0, z).start()
    share(0, z).start()
    outw.start()

    lanes = lax.broadcasted_iota(jnp.int32, (half // 2, 128), 1)
    for i in range(n):
        raw = qbox[i].astype(F32) * 0.125
        qs[i * half : i * half + half // 2, :] = jnp.where(lanes < HD, raw, 0.0).astype(BF16)
        qs[i * half + half // 2 : (i + 1) * half, :] = jnp.where(
            lanes < HD, pltpu.roll(raw, HD, 1), 0.0
        ).astype(BF16)

    total = qs.shape[0]
    def process(zz, core):
        pairs = kv[zz, core]
        s = lax.dot_general(qs[...], pairs, (((1,), (1,)), ((), ())), preferred_element_type=F32)
        old = m[...]
        new = jnp.maximum(old, jnp.max(s, axis=1, keepdims=True))
        m[...] = new
        decay = jnp.exp(old - new)
        w = jnp.exp(s - jnp.concatenate([new] * (width // 128), axis=1))
        part = w[:, 0:128]
        for piece in range(1, width // 128):
            part = part + w[:, piece * 128 : (piece + 1) * 128]
        l[...] = l[...] * decay + part
        acc[...] = acc[...] * decay + jnp.dot(w.astype(BF16), pairs, preferred_element_type=F32)

    def both(zz, other, core):
        def turn(i, carry):
            process(jnp.where(i == 0, zz, other), core)
            return carry

        lax.fori_loop(0, 2, turn, 0)

    kvw.pass_on(1)
    kvw.pass_on(2)
    process(z, c)
    taken(0, z).wait_recv()
    process(z, 1 - c)
    far = Z // 2
    for t in range(1, far + 1):
        below = lax.rem(z + Z - t, Z)
        above = lax.rem(z + t, Z)
        send_up(t - 1, below).wait_recv()
        if t < far:
            send_up(t, below).start()
            share(2 * t - 1, below).start()
        send_down(t - 1, above).wait_recv()
        if t < far:
            send_down(t, above).start()
            share(2 * t, above).start()
        else:
            share(2 * t - 1, below).start()
        if t == 1:
            kvw.arrive(3)
            kvw.arrive(4)
        if t < far:
            both(below, above, c)
        else:
            process(below, c)
        if t == 1:
            for k in (1, 2):
                proj_y.arrive(k)
                proj_z.arrive(k)
        if t == 2:
            kvw.arrive(5)
            kvw.arrive(6)
            for k in (3, 4):
                proj_y.arrive(k)
                proj_z.arrive(k)
            proj_y.pass_on(0)
        if t == 3:
            for k in (5, 6):
                proj_y.arrive(k)
                proj_z.arrive(k)
            kvw.arrive(7)
            outw.relay()
        taken(2 * t - 1, below).wait_recv()
        if t < far:
            taken(2 * t, above).wait_recv()
            both(below, above, 1 - c)
        else:
            process(below, 1 - c)
        if t == 2:
            kvw.pass_on(3)
            kvw.pass_on(4)
            proj_y.pass_on(1)
            proj_y.pass_on(2)
        if t == 3:
            proj_y.arrive(7)
            proj_z.arrive(7)
            proj_y.pass_on(3)
            proj_y.pass_on(4)
            kvw.pass_on(5)

    quarter = half // 4
    low = lax.broadcasted_iota(jnp.int32, (quarter // 2, 128), 1) < HD
    head = (x_hi * 2 + x_lo) * n + y

    def give(j, q, slot, sem):
        k = 4 * j + q
        return remote(obuf.at[k], abox.at[slot], a_s.at[k], a_r.at[sem], device(j, q // 2, q % 2, z, c))

    for j in range(n):
        for q in range(4):
            k = 4 * j + q
            at = j * half + q * quarter
            top, bot = pl.ds(at, quarter // 2), pl.ds(at + quarter // 2, quarter // 2)
            first = pltpu.roll(acc[top, :] / jnp.sum(l[top, :], axis=1, keepdims=True), HD, 1)
            second = acc[bot, :] / jnp.sum(l[bot, :], axis=1, keepdims=True)
            obuf[k] = jnp.where(low, first, second).astype(BF16)
    for j in range(n):
        for q in range(4):
            own = jnp.logical_and(mirror, jnp.logical_and(y == j, me == q))

            @pl.when(jnp.logical_not(own))
            def _():
                give(j, q, head, head).start()

            @pl.when(own)
            def _():
                pltpu.make_async_copy(obuf.at[4 * j + q], abox.at[head], loc.at[0]).start()


    for t in range(far):
        send_up(t, z).wait_send()
        send_down(t, z).wait_send()
    for k in range(2 * far):
        share(k, z).wait_send()
    outw.finish()
    own_w.wait()

    for h in range(4 * n):
        own = jnp.logical_and(mirror, head == h)

        @pl.when(jnp.logical_not(own))
        def _():
            remote(obuf.at[h], abox.at[h], a_s.at[h], a_r.at[h], twin).wait_recv()

        @pl.when(own)
        def _():
            pltpu.make_async_copy(obuf.at[h], abox.at[h], loc.at[0]).wait()

    for pair in range(2 * n):
        a = abox[2 * pair].astype(F32)
        b = abox[2 * pair + 1].astype(F32)
        cols = slice(pair * 128, (pair + 1) * 128)
        att[0 : quarter // 2, cols] = jnp.where(low, a, pltpu.roll(b, HD, 1)).astype(BF16)
        att[quarter // 2 :, cols] = jnp.where(low, pltpu.roll(a, HD, 1), b).astype(BF16)

    mixed = jnp.dot(
        att[...], owf[...].reshape(4 * ow.shape[0], ow.shape[1]), preferred_element_type=F32
    )
    tokens = quarter // 2
    pieces = []
    mine = pl.ds(pl.multiple_of(me * quarter, quarter), quarter)
    own_rows = jnp.concatenate([hbox[k, mine, :].astype(F32) for k in range(4)], axis=1)
    gain = jnp.concatenate([gf[k, 1:2, :] for k in range(4)], axis=1)
    for k in range(D // 128):
        at = slice(k * 128, (k + 1) * 128)
        res[k] = own_rows[:, at] + mixed[:, at]
        pieces.append(
            (res.at[k][pl.ds(0, tokens, stride=2), :] + res.at[k][pl.ds(1, tokens, stride=2), :]) * 0.5
        )
    pooled = jnp.concatenate(pieces, axis=1)
    pbox[x_lo, me] = normal(pooled, gain).astype(BF16)
    side = device(y, x_hi, c, z, 1 - x_lo)

    def lend(b):
        return remote(pbox.at[b, me], pbox.at[b, me], e_s.at[0], e_r.at[0], side)

    lend(x_lo).start()
    gather = Across(pbox.at[x_lo, me], pbox.at[x_lo], pb_s, pb_r)
    gather.start()
    lend(1 - x_lo).wait_recv()
    beside = Across(pbox.at[1 - x_lo, me], pbox.at[1 - x_lo], pc_s, pc_r)
    beside.start()
    for k in (5, 6, 7):
        proj_y.pass_on(k)
    gather.relay()
    kvw.pass_on(6)
    kvw.pass_on(7)
    proj_y.finish()
    proj_z.finish()
    gather.finish()

    def embed(b):
        post = pbox[b].reshape(4 * tokens, pbox.shape[3])
        weight = jnp.concatenate([pwy[...], pwz[...]], axis=2).reshape(2 * Z * pw.shape[0], pw.shape[1])
        return jnp.dot(post, weight, preferred_element_type=F32).astype(BF16).astype(F32)

    widened = embed(x_lo)
    sbox[me] = jnp.broadcast_to(
        jnp.sum(widened * widened, axis=1, keepdims=True), (4 * tokens, 128)
    )
    squares = Across(sbox.at[me], sbox, sb_s, sb_r)
    squares.start()
    ebox[x_lo] = (widened * rg[0:1, :]).astype(BF16)
    beside.relay()

    def hand(src):
        return remote(src, precv, e_s.at[1], e_r.at[1], side)

    def swap(k):
        return remote(tsend.at[k], trecv.at[k], t_s.at[k], t_r.at[k], twin)

    def over(k):
        return remote(csend.at[k], crecv.at[k], c_s.at[k], c_r.at[k], far_dev)

    kvw.finish()
    cols = pw.shape[1]
    part_c = cols // 2

    def columns(rows, a, b):
        at = pl.ds(pl.multiple_of((a * 2 + b) * part_c, part_c), part_c)
        return jnp.dot(ebox[rows], kwf[:, :, :, at].reshape(cols, part_c), preferred_element_type=F32)

    for k in range(2):
        rows = x_lo if k == 0 else 1 - x_lo
        if k == 1:
            beside.finish()
            ebox[rows] = (embed(rows) * rg[0:1, :]).astype(BF16)
        tsend[k, 0] = columns(rows, 1 - x_hi, 1 - c).astype(BF16)
        tsend[k, 1] = columns(rows, x_hi, 1 - c).astype(BF16)
        swap(k).start()
        keep[k, 0] = columns(rows, 1 - x_hi, c)
        keep[k, 1] = columns(rows, x_hi, c)
        if k == 0:
            squares.relay()
        swap(k).wait_recv()
        csend[k] = (keep[k, 0] + trecv[k, 0].astype(F32)).astype(BF16)
        over(k).start()
        keep[k, 1] = keep[k, 1] + trecv[k, 1].astype(F32)
    squares.finish()
    scale = lax.rsqrt((sbox[0] + sbox[1] + sbox[2] + sbox[3]) / DL + 1e-06)

    def turned(value, h, base):
        value = value * scale
        at = pl.ds(pl.multiple_of(base + h * LHD, LHD), LHD)
        out[:, at] = (value * cs[...] + pltpu.roll(value, HD, 1) * sn[...]).astype(BF16)

    heads_half = part_c // LHD
    over(0).wait_recv()
    for h in range(heads_half):
        at = slice(h * LHD, (h + 1) * LHD)
        turned(keep[0, 1, :, at] + crecv[0, :, at].astype(F32), h, x_lo * part_c)
    over(1).wait_recv()
    psend[...] = (keep[1, 1] + crecv[1].astype(F32)).astype(BF16)
    hand(psend).start()
    hand(psend).wait_recv()
    for h in range(heads_half):
        at = slice(h * LHD, (h + 1) * LHD)
        turned(precv[:, at].astype(F32), h, (1 - x_lo) * part_c)

    lend(x_lo).wait_send()
    hand(psend).wait_send()
    over(1).wait_send()
    edge_next.wait_send()
    edge_prev.wait_send()
    swap(0).wait_send()
    swap(1).wait_send()
    over(0).wait_send()
    for j in range(n):
        for q in range(4):
            own = jnp.logical_and(mirror, jnp.logical_and(y == j, me == q))

            @pl.when(jnp.logical_not(own))
            def _():
                give(j, q, head, head).wait_send()


def layer(mel, w1, c2, gn, qw, ow, pw, kw, rg, cs, sn):
    frames = mel.shape[0]
    n = lax.axis_size("tm")
    Z = lax.axis_size("section") // 2
    total = frames * n
    tokens = frames // 2
    quarter = frames // 4
    cols = pw.shape[1]
    wide = w1.shape[1]
    sem = pltpu.SemaphoreType.DMA
    vm = pl.BlockSpec(memory_space=pltpu.VMEM)
    V = pltpu.VMEM
    half = Z // 2
    ring = [sem((half,))] * 8 + [sem((Z,))] * 2
    return pl.pallas_call(
        layer_kernel,
        out_shape=jax.ShapeDtypeStruct((tokens, cols), BF16),
        in_specs=[vm] * 7 + [pl.BlockSpec(memory_space=pl.ANY)] + [vm] * 3,
        out_specs=vm,
        scratch_shapes=[
            V((16, mel.shape[1]), BF16),
            V((16, mel.shape[1]), BF16),
            V((4,) + w1.shape, BF16),
            V((4,) + gn.shape, F32),
            V((Z, 2, c2.shape[0] - BY_Y, wide), BF16),
            V((Z, 2, BY_Y, wide), BF16),
            V((Z, 2, ROWS_Y, qw.shape[1]), BF16),
            V((Z, 2, qw.shape[0] - ROWS_Y, qw.shape[1]), BF16),
            V((2, kw.shape[0], kw.shape[1] // 2), BF16),
            V((frames + 32, mel.shape[1]), F32),
            V((4, frames, wide), BF16),
            V((4, frames + 16, wide), F32),
            V((4, frames, wide), BF16),
            V((4, frames, wide), BF16),
            V((n, frames + tokens, 128), BF16),
            V((Z, 2, total, 128), BF16),
            V((n, tokens, 128), BF16),
            V((total, 128), BF16),
            V((total, 128), F32),
            V((total, 128), F32),
            V((total, 128), F32),
            V((16, quarter // 2, 128), BF16),
            V((16, quarter // 2, 128), BF16),
            V((quarter, ow.shape[0] * 4), BF16),
            V((ow.shape[1] // 128, quarter, 128), F32),
            V((4,) + ow.shape, BF16),
            V((Z, 2, ROWS_Y, cols), BF16),
            V((Z, 2, pw.shape[0] - ROWS_Y, cols), BF16),
            V((Z, 2, kw.shape[0], kw.shape[1] // 2), BF16),
            V((2, 4, quarter // 2, ow.shape[1]), BF16),
            V((4, tokens, 128), F32),
            V((2, tokens, cols), BF16),
            V((2, 2, tokens, cols // 2), F32),
            V((2, 2, tokens, cols // 2), BF16),
            V((2, 2, tokens, cols // 2), BF16),
            V((2, tokens, cols // 2), BF16),
            V((2, tokens, cols // 2), BF16),
            V((tokens, cols // 2), BF16),
            V((tokens, cols // 2), BF16),
            sem((n,)), sem((n,)), sem((n,)), sem((n,)), sem((20,)),
            sem((half,)), sem((half,)), sem((half,)), sem((half,)), sem((Z,)), sem((Z,)), sem((16,)), sem((16,)),
            sem((3,)), sem((3,)), sem((3,)), sem((3,)), sem((3,)), sem((3,)), sem((2,)), sem((2,)), sem((2,)), sem((2,)), sem((2,)), sem((2,)), sem((3,)), sem((3,)),
            sem((2,)), sem((2,)), sem((3,)), sem((3,)), sem((3,)), sem((3,)), sem((3,)), sem((3,)),
        ]
        + ring
        + ([sem((half,))] * 4 + [sem((1,))] * 2 + [sem((Z,))] * 8) * 4
        + ([sem((half,))] * 4 + [sem((1,))] * 2) * 2,
        compiler_params=pltpu.CompilerParams(
            collective_id=1, has_side_effects=True, vmem_limit_bytes=60 * 2**20
        ),
    )(mel, w1, c2, gn, qw, ow, pw, kw, rg, cs, sn)


def tables(rows, cols):
    row_start = (lax.axis_index("tm") * lax.axis_size("section") + lax.axis_index("section")) * rows
    positions = (row_start + jnp.arange(rows, dtype=jnp.int32)).astype(F32)
    within = jnp.arange(LHD, dtype=jnp.int32)
    freq = jnp.power(10000.0, -2.0 * (within % (LHD // 2)).astype(F32) / LHD)
    angle = positions[:, None] * freq[None, :]
    keys = lax.axis_index("mp") * cols < KVH * LHD
    sines = jnp.where(within < LHD // 2, -1.0, 1.0) * jnp.sin(angle)
    return jnp.where(keys, jnp.cos(angle), 1.0), jnp.where(keys, sines, 0.0)


def shards(
    mel_frames,
    conv1_weight,
    conv2_weight,
    attn_gain,
    qkv_weight,
    out_weight,
    post_gain,
    proj_weight,
    rms_gain,
    kv_weight,
):
    frames = mel_frames.shape[0] // 2
    bins, wide = conv1_weight.shape[1:]
    rows, _, width = qkv_weight.shape
    heads = width // HD
    split = qkv_weight.reshape(rows, 3, heads, HD)
    pairs = jnp.stack([split[:, 1], split[:, 2]], axis=2).reshape(rows, 2 * width)
    weight = jnp.concatenate([pairs, qkv_weight[:, 0]], axis=1)
    gains = jnp.pad(jnp.stack([attn_gain, post_gain]), ((0, 6), (0, 0)))
    cs, sn = tables(frames // 2, proj_weight.shape[1])
    return layer(
        mel_frames.reshape(frames, 2 * bins),
        conv1_weight.reshape(3 * bins, wide),
        conv2_weight.reshape(-1, wide),
        gains,
        weight,
        out_weight,
        proj_weight,
        kv_weight,
        rms_gain.reshape(1, -1),
        cs,
        sn,
    )


def solution(mesh):
    return jax.shard_map(
        shards,
        mesh=mesh,
        in_specs=(
            P(("tm", "section"), None),
            P(None, None, "mp"),
            P(None, "section", "mp"),
            P("mp"),
            P("section", None, "mp"),
            P("mp", None),
            P("mp"),
            P("section", "mp"),
            P("mp"),
            P(("mp", "section"), None),
        ),
        out_specs=P(("tm", "section"), "mp"),
        check_vma=False,
    )
```
